32 devices in a mesh: resp: 16 (over z, y, x), head: 2 (over core).
Axes of the slice: x: 2, y: 2, z: 4, core: 2. Of those that a mesh axis runs over, the one named last changes fastest.
Arguments:
- queries: bfloat16 [2048, 24576], P('resp', 'head'), may hold values from -8 to 8
- resp_latent: bfloat16 [2048, 576], P('resp'), may hold values from -8 to 8
- prompt_latent: bfloat16 [16, 32, 576], P('resp'), may hold values from -6 to 6
- up_keys: bfloat16 [128, 128, 512], P('head', None, 'resp'), may hold values from -0.5 to 0.5
- up_values: bfloat16 [128, 512, 128], P('head', 'resp'), may hold values from -0.25 to 0.25
- cotangent: bfloat16 [2048, 16384], P('resp', 'head'), may hold values from -6 to 6
- prompt_len: int32 [8], replicated, may hold values from 8 to 32
- resp_len: int32 [32], replicated, may hold values from 16 to 64
- resp_count: int32 [8], replicated, may hold values from 1 to 8, 32 in all
- owner: int32 [8], replicated, may hold values from 0 to 15, as said below
Outputs:
- attended: bfloat16 [2048, 16384], P('resp', 'head')
- grad_queries: bfloat16 [2048, 24576], P('resp', 'head')
- grad_response: float32 [2048, 576], P('resp', 'head')
- grad_prompt: float32 [16, 32, 576], P('resp', None, 'head')
The draws below stay inside these ranges and needn't reach their ends.
Inputs may be any that keep to these rules, and one draw needn't show every extreme that they name: Distinct slots; prompt p's cache is prompt_latent[owner[p]]. `resp_count`: every prompt has at least one response; they sum to 32.
All inputs are finite; a program needn't handle non-finite values.
Results may differ from the reference program's by a relative error of at most 0.014.
Values may be sent and summed in bfloat16 or wider, within the bound.
A program may use at most 128 MiB of HBM per device.

```python
import math
import jax
import jax.numpy as jnp
import numpy as np
from jax import lax

HEADS = 128
D_LAT = 512
D_ROPE = 64
D_NOPE = 128
D_VAL = 128
RL = 64
PLEN = 32
NPROMPT = 8
NRESP = 32
MOST = 8
TOKENS = 2048
N_RESP = 16


def draw_owner(key, part):
    shuffled = jax.random.permutation(jax.random.fold_in(key, 7), N_RESP)
    return shuffled[:NPROMPT].astype(jnp.int32)


def draw_queries(key, part):
    query_width = D_NOPE + D_ROPE
    sampled = jax.random.truncated_normal(jax.random.fold_in(key, 1), -6.0, 6.0, (TOKENS, HEADS, query_width), jnp.float32)
    return sampled.reshape(TOKENS, HEADS * query_width).astype(jnp.bfloat16)


def draw_resp_latent(key, part):
    sampled = jax.random.truncated_normal(jax.random.fold_in(key, 2), -6.0, 6.0, (TOKENS, D_LAT + D_ROPE), jnp.float32)
    return sampled.astype(jnp.bfloat16)


def with_ends(drawn, own_key, low, top_value):
    index_at = [jax.random.randint(jax.random.fold_in(own_key, axis), (), 0, length) for axis, length in enumerate(drawn.shape)]
    widest = drawn.shape.index(max(drawn.shape))
    neighbour = index_at[:widest] + [(index_at[widest] + 1) % drawn.shape[widest]] + index_at[widest + 1:]
    return drawn.at[tuple(index_at)].set(low).at[tuple(neighbour)].set(top_value)


def shard_levels(key, shape, pieces, least, top_value):
    def one(dim, shards_of):
        draws = jax.random.uniform(jax.random.fold_in(jax.random.fold_in(key, 6), dim), (shards_of,), jnp.float32, least / len(pieces), top_value / len(pieces))
        return jnp.repeat(jnp.exp(draws), shape[dim] // shards_of).reshape((-1,) + (1,) * (len(shape) - dim - 1))

    factor_of = one(*pieces[0])
    for cut in pieces[1:]:
        factor_of = factor_of * one(*cut)
    return factor_of


def length_profile(count, total, reach, slope):
    portions = [(1 << 20) // math.isqrt(standing ** slope) + 1 for standing in range(2, count + 1)]
    rest, given = total - reach - (count - 1), [1] * (count - 1)
    while rest > 0:
        movable = [i for i in range(count - 1) if given[i] < reach]
        pool, left = sum([portions[i] for i in movable]), rest
        for i in movable:
            addition = min(reach - given[i], max(1, left * portions[i] // pool), rest)
            given[i] = given[i] + addition
            rest = rest - addition
    return np.array([reach] + given)


def uneven(rng, number_of, total, most, lean):
    if number_of == 2:
        one = jax.random.randint(rng, (), max(1, total - most), min(most, total - 1) + 1)
        return jnp.stack([one, total - one])
    lengths = jnp.asarray(length_profile(number_of, total, most, lean), jnp.int32)
    pairs = (number_of - 1) // 2
    source_of, taker = lengths[1:1 + 2 * pairs:2], lengths[2:2 + 2 * pairs:2]
    room = jnp.minimum(source_of - 1, most - taker)
    shifted = jax.random.randint(jax.random.fold_in(rng, 1), (pairs,), 0, 1 << 20) % (room + 1)
    lengths = lengths.at[1:1 + 2 * pairs:2].set(source_of - shifted).at[2:2 + 2 * pairs:2].set(taker + shifted)
    return lengths[jax.random.permutation(jax.random.fold_in(rng, 2), number_of)]


def gaussian(rng, dims, scale, reach, shards=(), kind=jnp.bfloat16):
    result = scale * jax.random.normal(rng, dims, jnp.float32)
    if shards:
        result = result * shard_levels(rng, dims, shards, -0.22, 0.18)
    return jnp.clip(result, -reach, reach).astype(kind)


def setup_inputs(seed: int = 0) -> dict:
    arg_keys = jax.random.split(jax.random.key(seed), 11)
    queries = draw_queries(jax.random.fold_in(arg_keys[10], 71), 0)
    resp_latent = draw_resp_latent(jax.random.fold_in(arg_keys[10], 71), 0)
    prompt_latent = gaussian(arg_keys[2], (N_RESP, PLEN, D_LAT + D_ROPE), 1.0, 6.0, ((0, 16),))
    up_keys = gaussian(arg_keys[3], (HEADS, D_NOPE, D_LAT), D_NOPE ** -0.5, 0.5, ((0, 2), (2, 16)))
    up_values = gaussian(arg_keys[4], (HEADS, D_LAT, D_VAL), D_LAT ** -0.5, 0.25, ((0, 2), (1, 16)))
    cotangent = gaussian(arg_keys[5], (TOKENS, HEADS * D_VAL), 1.0, 6.0, ((0, 16), (1, 2)))
    prompt_len = with_ends(jax.random.randint(arg_keys[6], (NPROMPT,), PLEN // 4, PLEN + 1), jax.random.fold_in(arg_keys[6], 1), PLEN // 4, PLEN).astype(jnp.int32)
    resp_len = with_ends(jax.random.randint(arg_keys[7], (NRESP,), RL // 4, RL + 1), jax.random.fold_in(arg_keys[7], 1), RL // 4, RL).astype(jnp.int32)
    resp_count = uneven(arg_keys[8], NPROMPT, NRESP, MOST, 2).astype(jnp.int32)
    owner = draw_owner(jax.random.fold_in(arg_keys[10], 71), 0)
    return {"queries": queries, "resp_latent": resp_latent, "prompt_latent": prompt_latent, "up_keys": up_keys, "up_values": up_values, "cotangent": cotangent, "prompt_len": prompt_len, "resp_len": resp_len, "resp_count": resp_count, "owner": owner}


def product(form, left, right):
    return jnp.einsum(form, left.astype(jnp.float32), right.astype(jnp.float32))

def attend(queries, key_rows, key_valid, row_live, cotangent, up_keys, up_values):
    head_count, nope_width, latent_width = up_keys.shape
    row_count = queries.shape[0]
    split_query = queries.reshape(row_count, head_count, -1)
    score_scale = 1.0 / math.sqrt(split_query.shape[2])
    query_latent = product('thn,hnc->thc', split_query[:, :, :nope_width], up_keys).astype(jnp.bfloat16)
    query_full = jnp.concatenate([query_latent, split_query[:, :, nope_width:]], axis=2)
    scores = product('thc,kc->thk', query_full, key_rows) * score_scale
    scores = jnp.where(key_valid[:, None, :], scores, -jnp.inf)
    row_max = lax.optimization_barrier(jnp.max(scores, axis=2, keepdims=True))
    expo = jnp.exp(scores - row_max)
    weights = expo / lax.optimization_barrier(jnp.sum(expo, axis=2, keepdims=True))
    weights_bf = weights.astype(jnp.bfloat16)
    value_rows = key_rows[:, :latent_width]
    latent_out = product('thk,kc->thc', weights_bf, value_rows).astype(jnp.bfloat16)
    attended = product('thc,hcv->thv', latent_out, up_values) * row_live[:, None, None]
    grad_out = cotangent.reshape(row_count, head_count, -1)
    grad_latent = (product('thv,hcv->thc', grad_out, up_values) * row_live[:, None, None]).astype(jnp.bfloat16)
    grad_weights = product('thc,kc->thk', grad_latent, value_rows)
    inner = lax.optimization_barrier(jnp.sum(weights * grad_weights, axis=2, keepdims=True))
    grad_scores = (weights * (grad_weights - inner) * score_scale).astype(jnp.bfloat16)
    grad_full = product('thk,kc->thc', grad_scores, key_rows)
    grad_nope = product('thc,hnc->thn', grad_full[:, :, :latent_width].astype(jnp.bfloat16), up_keys)
    grad_query = jnp.concatenate([grad_nope, grad_full[:, :, latent_width:]], axis=2)
    grad_key = product('thk,thc->kc', grad_scores, query_full)
    grad_value = product('thk,thc->kc', weights_bf, grad_latent)
    grad_key = grad_key + jnp.pad(grad_value, ((0, 0), (0, key_rows.shape[1] - latent_width)))
    return (attended.reshape(row_count, -1).astype(jnp.bfloat16), grad_query.reshape(row_count, -1).astype(jnp.bfloat16), grad_key)

def reference(queries, resp_latent, prompt_latent, up_keys, up_values, cotangent, prompt_len, resp_len, resp_count, owner):
    resp_total = resp_len.shape[0]
    row_count = queries.shape[0] // resp_total
    prompt_rows = prompt_latent.shape[1]
    starts = jnp.cumsum(resp_count) - resp_count
    numbers = jnp.arange(resp_total, dtype=jnp.int32)
    prompt_of = lax.optimization_barrier(jnp.sum((starts[None, :] <= numbers[:, None]).astype(jnp.int32), axis=1)) - 1
    chosen = prompt_of[:, None] == jnp.arange(prompt_len.shape[0], dtype=jnp.int32)[None, :]
    slot_of = lax.optimization_barrier(jnp.sum(jnp.where(chosen, owner[None, :], 0), axis=1)).astype(jnp.int32)
    plen_of = lax.optimization_barrier(jnp.sum(jnp.where(chosen, prompt_len[None, :], 0), axis=1)).astype(jnp.int32)
    positions = jnp.arange(row_count, dtype=jnp.int32)
    prompt_pos = jnp.arange(prompt_rows, dtype=jnp.int32)
    causal = positions[:, None] >= positions[None, :]

    def one_response(carry, number):
        start = (number * row_count).astype(jnp.int32)
        query_rows = lax.dynamic_slice_in_dim(queries, start, row_count, 0)
        own_rows = lax.dynamic_slice_in_dim(resp_latent, start, row_count, 0)
        grad_rows = lax.dynamic_slice_in_dim(cotangent, start, row_count, 0)
        slot = slot_of[number]
        prompt_rows_now = lax.dynamic_index_in_dim(prompt_latent, slot, 0, keepdims=False)
        key_rows = jnp.concatenate([prompt_rows_now, own_rows], axis=0)
        prompt_ok = jnp.broadcast_to(prompt_pos[None, :] < plen_of[number], (row_count, prompt_rows))
        key_valid = jnp.concatenate([prompt_ok, causal], axis=1)
        row_live = (positions < resp_len[number]).astype(jnp.float32)
        attended, grad_query, grad_key = attend(query_rows, key_rows, key_valid, row_live, grad_rows, up_keys, up_values)
        carry = carry.at[slot].add(grad_key[:prompt_rows])
        return (carry, (attended, grad_query, grad_key[prompt_rows:]))
    empty = jnp.zeros(prompt_latent.shape, jnp.float32)
    grad_prompt, (attended, grad_queries, grad_response) = lax.scan(one_response, empty, numbers)
    return (attended.reshape(queries.shape[0], -1), grad_queries.reshape(queries.shape[0], -1), grad_response.reshape(queries.shape[0], -1), grad_prompt)
```

```python
import functools
import math

import jax
import jax.numpy as jnp
from jax import lax
from jax.experimental import pallas as pl
from jax.experimental.pallas import tpu as pltpu
from jax.sharding import PartitionSpec as P

MESH = pl.DeviceIdType.MESH
NT = (((1,), (1,)), ((), ()))
NN = (((1,), (0,)), ((), ()))
TN = (((0,), (0,)), ((), ()))


def mm(left, right, form):
    return lax.dot_general(left, right, form, preferred_element_type=jnp.float32)


def kernel(
    line,
    chunks,
    heads_per,
    resp_per,
    meta,
    q_ref,
    cot_ref,
    w_ref,
    prompt_ref,
    resp_ref,
    att_ref,
    gq_ref,
    gk_ref,
    full,
    prompts,
    keys,
    qf,
    gl,
    lo,
    gf,
    own_sem,
    line_send,
    line_recv,
    pair_send,
    pair_recv,
):
    step = pl.program_id(0)
    me = lax.axis_index("resp")
    x = lax.rem(me, 2)
    y = lax.rem(lax.div(me, 2), 2)
    z = lax.div(me, 4)

    def at(zz, yy, xx):
        return {"resp": (zz * 2 + yy) * 2 + xx}

    y_peer, x_peer = at(z, 1 - y, x), at(z, y, 1 - x)

    def remote(src, dst, send, recv, peer):
        return pltpu.make_async_remote_copy(
            src_ref=src, dst_ref=dst, send_sem=send, recv_sem=recv, device_id=peer, device_id_type=MESH
        )

    def heads(c):
        return pl.ds(c * heads_per, heads_per)

    def own_copy(c):
        return pltpu.make_async_copy(
            w_ref.at[:, heads(c)], full.at[:, z, y, x, heads(c)], own_sem.at[c]
        )

    def line_copy(c, d, source):
        return remote(
            w_ref.at[:, heads(c)],
            full.at[:, source, y, x, heads(c)],
            line_send.at[c, d - 1],
            line_recv.at[c, d - 1],
            at(lax.rem(z + d, line), y, x),
        )

    def pair_copies(c, yy, xx):
        first_k = full.at[0, :, yy[0], xx[0], heads(c)]
        first_v = full.at[1, :, yy[1], xx[1], heads(c)]
        second_k = full.at[0, :, :, xx[2], heads(c)]
        second_v = full.at[1, :, yy[2], :, heads(c)]
        refs = ((first_k, y_peer), (first_v, x_peer), (second_k, x_peer), (second_v, y_peer))
        return [
            remote(ref, ref, pair_send.at[c, i], pair_recv.at[c, i], peer)
            for i, (ref, peer) in enumerate(refs)
        ]

    def out_pairs(c):
        return pair_copies(c, (y, y, y), (x, x, x))

    def in_pairs(c):
        return pair_copies(c, (1 - y, y, 1 - y), (x, 1 - x, 1 - x))

    def own_prompt():
        return pltpu.make_async_copy(prompt_ref.at[0], prompts.at[z, y, x], own_sem.at[chunks])

    def line_prompt(d, source):
        return remote(
            prompt_ref.at[0],
            prompts.at[source, y, x],
            line_send.at[chunks, d - 1],
            line_recv.at[chunks, d - 1],
            at(lax.rem(z + d, line), y, x),
        )

    def prompt_pairs(yy, xx):
        refs = ((prompts.at[:, yy, x], y_peer), (prompts.at[:, :, xx], x_peer))
        return [
            remote(ref, ref, pair_send.at[chunks, i], pair_recv.at[chunks, i], peer)
            for i, (ref, peer) in enumerate(refs)
        ]

    @pl.when(step == 0)
    def _():
        barrier = pltpu.get_barrier_semaphore()
        for d in range(1, line):
            pl.semaphore_signal(
                barrier, inc=1, device_id=at(lax.rem(z + d, line), y, x), device_id_type=MESH
            )
        pl.semaphore_signal(barrier, inc=1, device_id=y_peer, device_id_type=MESH)
        pl.semaphore_signal(barrier, inc=1, device_id=x_peer, device_id_type=MESH)
        pl.semaphore_wait(barrier, line + 1)
        own_prompt().start()
        for d in range(1, line):
            line_prompt(d, z).start()
        gk_ref[...] = jnp.zeros_like(gk_ref)

    @pl.when(step < chunks)
    def _():
        own_copy(step).start()
        for d in range(1, line):
            line_copy(step, d, z).start()

    @pl.when(step == 1)
    def _():
        own_prompt().wait()
        for d in range(1, line):
            line_prompt(d, lax.rem(z + line - d, line)).wait_recv()
        prompt_pairs(y, x)[0].start()

    @pl.when((step >= 1) & (step < chunks + 1))
    def _():
        c = step - 1
        own_copy(c).wait()
        for d in range(1, line):
            line_copy(c, d, lax.rem(z + line - d, line)).wait_recv()
        sends = out_pairs(c)
        sends[0].start()
        sends[1].start()

    @pl.when(step == 2)
    def _():
        prompt_pairs(1 - y, 1 - x)[0].wait_recv()
        prompt_pairs(y, x)[1].start()

    @pl.when((step >= 2) & (step < chunks + 2))
    def _():
        c = step - 2
        arrivals, sends = in_pairs(c), out_pairs(c)
        arrivals[0].wait_recv()
        arrivals[1].wait_recv()
        sends[2].start()
        sends[3].start()

    plen_rows = prompt_ref.shape[1]
    tokens = resp_ref.shape[1]
    key_count, key_cols = keys.shape[1], keys.shape[2]
    latent = gl.shape[2]
    slice_cols, nope = w_ref.shape[2], w_ref.shape[3]
    value_cols = nope
    q_cols = q_ref.shape[1] // heads_per
    rows = heads_per * tokens
    scale = 1.0 / math.sqrt(q_cols)

    @pl.when(step == 3)
    def _():
        prompt_pairs(1 - y, 1 - x)[1].wait_recv()
        for r in range(resp_per):
            keys[r, :plen_rows, :] = prompts[meta[r, 0], meta[r, 1], meta[r, 2]]
            keys[r, plen_rows:, :] = resp_ref[r]

    @pl.when(step >= 3)
    def _():
        c = step - 3
        arrivals = in_pairs(c)
        arrivals[2].wait_recv()
        arrivals[3].wait_recv()

        def weight(kind, h):
            got = full[kind, :, :, :, c * heads_per + h]
            if slice_cols % 16:
                return got.astype(jnp.float32).reshape(latent, nope).astype(jnp.bfloat16)
            return got.reshape(latent, nope)

        token_row = lax.broadcasted_iota(jnp.int32, (resp_per * tokens, 1), 0)
        live = jnp.zeros((resp_per * tokens, 1), jnp.float32)
        for r in range(resp_per):
            inside = (token_row >= r * tokens) & (token_row < r * tokens + meta[r, 4])
            live = jnp.where(inside, 1.0, live)

        for h in range(heads_per):
            wk, wv = weight(0, h), weight(1, h)
            q_latent = mm(q_ref[:, h * q_cols : h * q_cols + nope], wk, NT).astype(jnp.bfloat16)
            rope = q_ref[:, h * q_cols + nope : (h + 1) * q_cols]
            grad_latent = mm(cot_ref[:, h * value_cols : (h + 1) * value_cols], wv, NT) * live
            grad_latent = grad_latent.astype(jnp.bfloat16)
            for r in range(resp_per):
                mine = slice(r * tokens, (r + 1) * tokens)
                place = slice(h * tokens, (h + 1) * tokens)
                qf[r, place, :latent] = q_latent[mine]
                qf[r, place, latent:] = rope[mine]
                gl[r, place, :] = grad_latent[mine]

        key_at = lax.broadcasted_iota(jnp.int32, (key_count, rows), 0)
        token_at = lax.rem(lax.broadcasted_iota(jnp.int32, (key_count, rows), 1), tokens)
        for r in range(resp_per):
            key = keys[r]
            value = key[:, :latent]
            query, grad_latent = qf[r], gl[r]
            scores = mm(key, query, NT) * scale
            last = jnp.where(key_at < plen_rows, meta[r, 3] - 1, token_at + plen_rows)
            scores = jnp.where(key_at <= last, scores, -jnp.inf)
            expo = jnp.exp(scores - jnp.max(scores, axis=0, keepdims=True))
            weights = expo / jnp.sum(expo, axis=0, keepdims=True)
            weights_bf = weights.astype(jnp.bfloat16)
            grad_weights = mm(value, grad_latent, NT)
            inner = jnp.sum(weights * grad_weights, axis=0, keepdims=True)
            grad_scores = (weights * (grad_weights - inner) * scale).astype(jnp.bfloat16)
            lo_r = mm(weights_bf, value, TN).astype(jnp.bfloat16)
            gf_r = mm(grad_scores, key, TN).astype(jnp.bfloat16)
            for h in range(heads_per):
                mine = slice(r * tokens, (r + 1) * tokens)
                place = slice(h * tokens, (h + 1) * tokens)
                lo[h, mine, :] = lo_r[place]
                gf[h, mine, :] = gf_r[place]
            gk_ref[r] += mm(grad_scores, query, NN)
            gk_ref[r, :, :latent] += mm(weights_bf, grad_latent, NN)

        for h in range(heads_per):
            wk, wv = weight(0, h), weight(1, h)
            attended = mm(lo[h], wv, NN) * live
            att_ref[:, h * value_cols : (h + 1) * value_cols] = attended.astype(jnp.bfloat16)
            grad_nope = mm(gf[h, :, :latent], wk, NN).astype(jnp.bfloat16)
            gq_ref[:, h * q_cols : h * q_cols + nope] = grad_nope
            gq_ref[:, h * q_cols + nope : (h + 1) * q_cols] = gf[h, :, latent:]

        sends = out_pairs(c)
        for i in range(4):
            sends[i].wait_send()
        for d in range(1, line):
            line_copy(c, d, z).wait_send()

    @pl.when(step == 3)
    def _():
        sends = prompt_pairs(y, x)
        sends[0].wait_send()
        sends[1].wait_send()
        for d in range(1, line):
            line_prompt(d, z).wait_send()


def fused(queries, cotangent, weights, prompt_latent, own_rows, meta, resp_devices):
    line = resp_devices // 4
    head_count, slice_cols, nope = weights.shape[1:]
    resp_per, tokens, key_cols = own_rows.shape
    prompt_rows = prompt_latent.shape[1]
    heads_per = math.gcd(4, head_count)
    chunks = head_count // heads_per
    row_count = queries.shape[0]
    q_cols = queries.shape[1] // head_count
    latent = slice_cols * resp_devices
    key_count = prompt_rows + tokens
    rows = heads_per * tokens
    bf = jnp.bfloat16

    def tile(t):
        return (0, lax.max(t - 3, 0))

    whole = pl.BlockSpec(memory_space=pltpu.VMEM)
    return pl.pallas_call(
        functools.partial(kernel, line, chunks, heads_per, resp_per),
        out_shape=(
            jax.ShapeDtypeStruct(cotangent.shape, bf),
            jax.ShapeDtypeStruct(queries.shape, bf),
            jax.ShapeDtypeStruct((resp_per, key_count, key_cols), jnp.float32),
        ),
        grid=(chunks + 3,),
        in_specs=[
            pl.BlockSpec(memory_space=pltpu.SMEM),
            pl.BlockSpec((row_count, heads_per * q_cols), tile),
            pl.BlockSpec((row_count, heads_per * nope), tile),
            whole,
            whole,
            whole,
        ],
        out_specs=(
            pl.BlockSpec((row_count, heads_per * nope), tile),
            pl.BlockSpec((row_count, heads_per * q_cols), tile),
            whole,
        ),
        scratch_shapes=[
            pltpu.VMEM((2, line, 2, 2, head_count, slice_cols, nope), bf),
            pltpu.VMEM((line, 2, 2, prompt_rows, key_cols), bf),
            pltpu.VMEM((resp_per, key_count, key_cols), bf),
            pltpu.VMEM((resp_per, rows, key_cols), bf),
            pltpu.VMEM((resp_per, rows, latent), bf),
            pltpu.VMEM((heads_per, resp_per * tokens, latent), bf),
            pltpu.VMEM((heads_per, resp_per * tokens, key_cols), bf),
            pltpu.SemaphoreType.DMA((chunks + 1,)),
            pltpu.SemaphoreType.DMA((chunks + 1, line - 1)),
            pltpu.SemaphoreType.DMA((chunks + 1, line - 1)),
            pltpu.SemaphoreType.DMA((chunks + 1, 4)),
            pltpu.SemaphoreType.DMA((chunks + 1, 4)),
        ],
        compiler_params=pltpu.CompilerParams(
            collective_id=0, has_side_effects=True, dimension_semantics=("arbitrary",)
        ),
    )(meta, queries, cotangent, weights, prompt_latent, own_rows)


def body(
    queries,
    resp_latent,
    prompt_latent,
    up_keys,
    up_values,
    cotangent,
    prompt_len,
    resp_len,
    resp_count,
    owner,
):
    resp_devices = lax.axis_size("resp")
    head_devices = lax.axis_size("head")
    my_index = lax.axis_index("resp")
    resp_total = resp_len.shape[0]
    per_device = resp_total // resp_devices
    row_count = queries.shape[0] // per_device
    prompt_rows = prompt_latent.shape[1]
    piece_rows = prompt_rows // resp_devices
    latent_cols = prompt_latent.shape[2]
    starts = jnp.cumsum(resp_count) - resp_count
    numbers = jnp.arange(resp_total, dtype=jnp.int32)
    prompt_of = jnp.sum((starts[None, :] <= numbers[:, None]).astype(jnp.int32), axis=1) - 1
    chosen = prompt_of[:, None] == jnp.arange(prompt_len.shape[0], dtype=jnp.int32)[None, :]
    slot_of = jnp.sum(jnp.where(chosen, owner[None, :], 0), axis=1)
    plen_of = jnp.sum(jnp.where(chosen, prompt_len[None, :], 0), axis=1)
    table = jnp.stack([slot_of // 4, (slot_of // 2) % 2, slot_of % 2, plen_of, resp_len], axis=1)
    meta = lax.dynamic_slice_in_dim(table, my_index * per_device, per_device)
    weights = jnp.stack([jnp.swapaxes(up_keys, 1, 2), up_values])
    own_rows = resp_latent.reshape(per_device, row_count, latent_cols)
    attended, grad_query, grad_key = fused(
        queries, cotangent, weights, prompt_latent, own_rows, meta, resp_devices
    )
    share = latent_cols // head_devices
    parts = grad_key.reshape(per_device, prompt_rows + row_count, head_devices, share)
    parts = jnp.moveaxis(parts, 2, 0).astype(jnp.bfloat16)
    parts = lax.all_to_all(parts, "head", split_axis=0, concat_axis=0, tiled=True)
    mine = jnp.sum(parts.astype(jnp.float32), axis=0)
    grad_own = mine[:, prompt_rows:].reshape(per_device * row_count, share)
    grad_prompt_rows = mine[:, :prompt_rows].astype(jnp.bfloat16)
    arrived = lax.all_to_all(
        grad_prompt_rows[None], "resp", split_axis=2, concat_axis=0, tiled=True
    ).astype(jnp.float32)
    flat_rows = arrived.reshape(resp_devices * per_device, piece_rows * share)
    slot_table = (slot_of[None, :] == jnp.arange(resp_devices, dtype=jnp.int32)[:, None]).astype(
        jnp.float32
    )
    summed = jnp.dot(slot_table, flat_rows, precision=lax.Precision.HIGHEST)
    summed = summed.reshape(resp_devices, piece_rows, share)
    at_owner = lax.all_to_all(
        summed.astype(jnp.bfloat16), "resp", split_axis=0, concat_axis=1, tiled=True
    ).astype(summed.dtype)
    return attended, grad_query, grad_own, at_owner


def solution(mesh):
    placed = (
        P("resp", "head"),
        P("resp", None),
        P("resp", None, None),
        P("head", None, "resp"),
        P("head", "resp", None),
        P("resp", "head"),
        P(),
        P(),
        P(),
        P(),
    )
    return jax.shard_map(
        body,
        mesh=mesh,
        in_specs=placed,
        out_specs=(
            P("resp", "head"),
            P("resp", "head"),
            P("resp", "head"),
            P("resp", None, "head"),
        ),
        check_vma=False,
    )
```

```python
import functools
import math

import jax
import jax.numpy as jnp
from jax import lax
from jax.experimental import pallas as pl
from jax.experimental.pallas import tpu as pltpu
from jax.sharding import PartitionSpec as P

MESH = pl.DeviceIdType.MESH
NT = (((1,), (1,)), ((), ()))
NN = (((1,), (0,)), ((), ()))
TN = (((0,), (0,)), ((), ()))


def mm(left, right, form):
    return lax.dot_general(left, right, form, preferred_element_type=jnp.float32)


def kernel(
    line,
    chunks,
    heads_per,
    resp_per,
    meta,
    q_ref,
    cot_ref,
    w_ref,
    prompt_ref,
    resp_ref,
    att_ref,
    gq_ref,
    parts_ref,
    gk_ref,
    full,
    prompts,
    keys,
    qf,
    gl,
    lo,
    gf,
    own_sem,
    line_send,
    line_recv,
    pair_send,
    pair_recv,
):
    step = pl.program_id(0)
    me = lax.axis_index("resp")
    x = lax.rem(me, 2)
    y = lax.rem(lax.div(me, 2), 2)
    z = lax.div(me, 4)

    def at(zz, yy, xx):
        return {"resp": (zz * 2 + yy) * 2 + xx}

    y_peer, x_peer = at(z, 1 - y, x), at(z, y, 1 - x)

    def remote(src, dst, send, recv, peer):
        return pltpu.make_async_remote_copy(
            src_ref=src, dst_ref=dst, send_sem=send, recv_sem=recv, device_id=peer, device_id_type=MESH
        )

    def heads(c):
        return pl.ds(c * heads_per, heads_per)

    def own_copy(c):
        return pltpu.make_async_copy(
            w_ref.at[:, heads(c)], full.at[:, z, y, x, heads(c)], own_sem.at[c]
        )

    def line_copy(c, d, source):
        return remote(
            w_ref.at[:, heads(c)],
            full.at[:, source, y, x, heads(c)],
            line_send.at[c, d - 1],
            line_recv.at[c, d - 1],
            at(lax.rem(z + d, line), y, x),
        )

    def pair_copies(c, yy, xx):
        first_k = full.at[0, :, yy[0], xx[0], heads(c)]
        first_v = full.at[1, :, yy[1], xx[1], heads(c)]
        second_k = full.at[0, :, :, xx[2], heads(c)]
        second_v = full.at[1, :, yy[2], :, heads(c)]
        refs = ((first_k, y_peer), (first_v, x_peer), (second_k, x_peer), (second_v, y_peer))
        return [
            remote(ref, ref, pair_send.at[c, i], pair_recv.at[c, i], peer)
            for i, (ref, peer) in enumerate(refs)
        ]

    def out_pairs(c):
        return pair_copies(c, (y, y, y), (x, x, x))

    def in_pairs(c):
        return pair_copies(c, (1 - y, y, 1 - y), (x, 1 - x, 1 - x))

    def own_prompt():
        return pltpu.make_async_copy(prompt_ref.at[0], prompts.at[z, y, x], own_sem.at[chunks])

    def line_prompt(d, source):
        return remote(
            prompt_ref.at[0],
            prompts.at[source, y, x],
            line_send.at[chunks, d - 1],
            line_recv.at[chunks, d - 1],
            at(lax.rem(z + d, line), y, x),
        )

    def prompt_pairs(yy, xx):
        refs = ((prompts.at[:, yy, x], y_peer), (prompts.at[:, :, xx], x_peer))
        return [
            remote(ref, ref, pair_send.at[chunks, i], pair_recv.at[chunks, i], peer)
            for i, (ref, peer) in enumerate(refs)
        ]

    @pl.when(step == 0)
    def _():
        barrier = pltpu.get_barrier_semaphore()
        for d in range(1, line):
            pl.semaphore_signal(
                barrier, inc=1, device_id=at(lax.rem(z + d, line), y, x), device_id_type=MESH
            )
        pl.semaphore_signal(barrier, inc=1, device_id=y_peer, device_id_type=MESH)
        pl.semaphore_signal(barrier, inc=1, device_id=x_peer, device_id_type=MESH)
        pl.semaphore_wait(barrier, line + 1)
        own_prompt().start()
        for d in range(1, line):
            line_prompt(d, z).start()
        gk_ref[...] = jnp.zeros_like(gk_ref)

    @pl.when(step < chunks)
    def _():
        own_copy(step).start()
        for d in range(1, line):
            line_copy(step, d, z).start()

    @pl.when(step == 1)
    def _():
        own_prompt().wait()
        for d in range(1, line):
            line_prompt(d, lax.rem(z + line - d, line)).wait_recv()
        prompt_pairs(y, x)[0].start()

    @pl.when((step >= 1) & (step < chunks + 1))
    def _():
        c = step - 1
        own_copy(c).wait()
        for d in range(1, line):
            line_copy(c, d, lax.rem(z + line - d, line)).wait_recv()
        sends = out_pairs(c)
        sends[0].start()
        sends[1].start()

    @pl.when(step == 2)
    def _():
        prompt_pairs(1 - y, 1 - x)[0].wait_recv()
        prompt_pairs(y, x)[1].start()

    @pl.when((step >= 2) & (step < chunks + 2))
    def _():
        c = step - 2
        arrivals, sends = in_pairs(c), out_pairs(c)
        arrivals[0].wait_recv()
        arrivals[1].wait_recv()
        sends[2].start()
        sends[3].start()

    plen_rows = prompt_ref.shape[1]
    tokens = resp_ref.shape[1]
    key_count, key_cols = keys.shape[1], keys.shape[2]
    latent = gl.shape[2]
    slice_cols, nope = w_ref.shape[2], w_ref.shape[3]
    value_cols = nope
    q_cols = q_ref.shape[1] // heads_per
    rows = heads_per * tokens
    scale = 1.0 / math.sqrt(q_cols)

    @pl.when(step == 3)
    def _():
        prompt_pairs(1 - y, 1 - x)[1].wait_recv()
        for r in range(resp_per):
            keys[r, :plen_rows, :] = prompts[meta[r, 0], meta[r, 1], meta[r, 2]]
            keys[r, plen_rows:, :] = resp_ref[r]

    @pl.when(step >= 3)
    def _():
        c = step - 3
        arrivals = in_pairs(c)
        arrivals[2].wait_recv()
        arrivals[3].wait_recv()

        def weight(kind, h):
            got = full[kind, :, :, :, c * heads_per + h]
            if slice_cols % 16:
                return got.astype(jnp.float32).reshape(latent, nope).astype(jnp.bfloat16)
            return got.reshape(latent, nope)

        token_row = lax.broadcasted_iota(jnp.int32, (resp_per * tokens, 1), 0)
        live = jnp.zeros((resp_per * tokens, 1), jnp.float32)
        for r in range(resp_per):
            inside = (token_row >= r * tokens) & (token_row < r * tokens + meta[r, 4])
            live = jnp.where(inside, 1.0, live)

        for h in range(heads_per):
            wk, wv = weight(0, h), weight(1, h)
            q_latent = mm(q_ref[:, h * q_cols : h * q_cols + nope], wk, NT).astype(jnp.bfloat16)
            rope = q_ref[:, h * q_cols + nope : (h + 1) * q_cols]
            grad_latent = mm(cot_ref[:, h * value_cols : (h + 1) * value_cols], wv, NT) * live
            grad_latent = grad_latent.astype(jnp.bfloat16)
            for r in range(resp_per):
                mine = slice(r * tokens, (r + 1) * tokens)
                place = slice(h * tokens, (h + 1) * tokens)
                qf[r, place, :latent] = q_latent[mine]
                qf[r, place, latent:] = rope[mine]
                gl[r, place, :] = grad_latent[mine]

        key_at = lax.broadcasted_iota(jnp.int32, (key_count, rows), 0)
        token_at = lax.rem(lax.broadcasted_iota(jnp.int32, (key_count, rows), 1), tokens)
        for r in range(resp_per):
            key = keys[r]
            value = key[:, :latent]
            query, grad_latent = qf[r], gl[r]
            scores = mm(key, query, NT) * scale
            last = jnp.where(key_at < plen_rows, meta[r, 3] - 1, token_at + plen_rows)
            scores = jnp.where(key_at <= last, scores, -jnp.inf)
            expo = jnp.exp(scores - jnp.max(scores, axis=0, keepdims=True))
            weights = expo / jnp.sum(expo, axis=0, keepdims=True)
            weights_bf = weights.astype(jnp.bfloat16)
            grad_weights = mm(value, grad_latent, NT)
            inner = jnp.sum(weights * grad_weights, axis=0, keepdims=True)
            grad_scores = (weights * (grad_weights - inner) * scale).astype(jnp.bfloat16)
            lo_r = mm(weights_bf, value, TN).astype(jnp.bfloat16)
            gf_r = mm(grad_scores, key, TN).astype(jnp.bfloat16)
            for h in range(heads_per):
                mine = slice(r * tokens, (r + 1) * tokens)
                place = slice(h * tokens, (h + 1) * tokens)
                lo[h, mine, :] = lo_r[place]
                gf[h, mine, :] = gf_r[place]
            gk_ref[r] += mm(grad_scores, query, NN)
            gk_ref[r, :, :latent] += mm(weights_bf, grad_latent, NN)

        for h in range(heads_per):
            wk, wv = weight(0, h), weight(1, h)
            attended = mm(lo[h], wv, NN) * live
            att_ref[:, h * value_cols : (h + 1) * value_cols] = attended.astype(jnp.bfloat16)
            grad_nope = mm(gf[h, :, :latent], wk, NN).astype(jnp.bfloat16)
            gq_ref[:, h * q_cols : h * q_cols + nope] = grad_nope
            gq_ref[:, h * q_cols + nope : (h + 1) * q_cols] = gf[h, :, latent:]

        sends = out_pairs(c)
        for i in range(4):
            sends[i].wait_send()
        for d in range(1, line):
            line_copy(c, d, z).wait_send()

    @pl.when(step == chunks + 2)
    def _():
        share = parts_ref.shape[3]
        for r in range(resp_per):
            for part in range(parts_ref.shape[0]):
                cut = gk_ref[r, :, part * share : (part + 1) * share]
                parts_ref[part, r] = cut.astype(jnp.bfloat16)

    @pl.when(step == 3)
    def _():
        sends = prompt_pairs(y, x)
        sends[0].wait_send()
        sends[1].wait_send()
        for d in range(1, line):
            line_prompt(d, z).wait_send()


def fused(queries, cotangent, weights, prompt_latent, own_rows, meta, resp_devices, head_devices):
    line = resp_devices // 4
    head_count, slice_cols, nope = weights.shape[1:]
    resp_per, tokens, key_cols = own_rows.shape
    prompt_rows = prompt_latent.shape[1]
    heads_per = math.gcd(4, head_count)
    chunks = head_count // heads_per
    row_count = queries.shape[0]
    q_cols = queries.shape[1] // head_count
    latent = slice_cols * resp_devices
    key_count = prompt_rows + tokens
    rows = heads_per * tokens
    bf = jnp.bfloat16

    def tile(t):
        return (0, lax.max(t - 3, 0))

    whole = pl.BlockSpec(memory_space=pltpu.VMEM)
    return pl.pallas_call(
        functools.partial(kernel, line, chunks, heads_per, resp_per),
        out_shape=(
            jax.ShapeDtypeStruct(cotangent.shape, bf),
            jax.ShapeDtypeStruct(queries.shape, bf),
            jax.ShapeDtypeStruct(
                (head_devices, resp_per, key_count, key_cols // head_devices), bf
            ),
        ),
        grid=(chunks + 3,),
        in_specs=[
            pl.BlockSpec(memory_space=pltpu.SMEM),
            pl.BlockSpec((row_count, heads_per * q_cols), tile),
            pl.BlockSpec((row_count, heads_per * nope), tile),
            whole,
            whole,
            whole,
        ],
        out_specs=(
            pl.BlockSpec((row_count, heads_per * nope), tile),
            pl.BlockSpec((row_count, heads_per * q_cols), tile),
            whole,
        ),
        scratch_shapes=[
            pltpu.VMEM((resp_per, key_count, key_cols), jnp.float32),
            pltpu.VMEM((2, line, 2, 2, head_count, slice_cols, nope), bf),
            pltpu.VMEM((line, 2, 2, prompt_rows, key_cols), bf),
            pltpu.VMEM((resp_per, key_count, key_cols), bf),
            pltpu.VMEM((resp_per, rows, key_cols), bf),
            pltpu.VMEM((resp_per, rows, latent), bf),
            pltpu.VMEM((heads_per, resp_per * tokens, latent), bf),
            pltpu.VMEM((heads_per, resp_per * tokens, key_cols), bf),
            pltpu.SemaphoreType.DMA((chunks + 1,)),
            pltpu.SemaphoreType.DMA((chunks + 1, line - 1)),
            pltpu.SemaphoreType.DMA((chunks + 1, line - 1)),
            pltpu.SemaphoreType.DMA((chunks + 1, 4)),
            pltpu.SemaphoreType.DMA((chunks + 1, 4)),
        ],
        compiler_params=pltpu.CompilerParams(
            collective_id=0, has_side_effects=True, dimension_semantics=("arbitrary",)
        ),
    )(meta, queries, cotangent, weights, prompt_latent, own_rows)


def tail_kernel(
    devices,
    head_devices,
    prompt_rows,
    slots,
    parts_ref,
    own_ref,
    prompt_out,
    head_in,
    out_rows,
    in_rows,
    out_sums,
    in_sums,
    head_send,
    head_recv,
    row_send,
    row_recv,
    sum_send,
    sum_recv,
):
    me = lax.axis_index("resp")
    mine = lax.axis_index("head")
    resp_per, key_count, share = parts_ref.shape[1:]
    tokens = key_count - prompt_rows
    piece = prompt_rows // devices

    def ahead(d):
        return lax.rem(me + d, devices)

    def behind(d):
        return lax.rem(me + devices - d, devices)

    barrier = pltpu.get_barrier_semaphore()
    for d in range(1, devices):
        pl.semaphore_signal(barrier, inc=1, device_id={"resp": ahead(d)}, device_id_type=MESH)
    for d in range(1, head_devices):
        peer = lax.rem(mine + d, head_devices)
        pl.semaphore_signal(barrier, inc=1, device_id={"head": peer}, device_id_type=MESH)
    pl.semaphore_wait(barrier, devices + head_devices - 2)

    def head_copy(d, slot):
        peer = lax.rem(mine + d, head_devices)
        return pltpu.make_async_remote_copy(
            src_ref=parts_ref.at[peer],
            dst_ref=head_in.at[slot],
            send_sem=head_send.at[d - 1],
            recv_sem=head_recv.at[d - 1],
            device_id={"head": peer},
            device_id_type=MESH,
        )

    def spread(source, target, send, recv, d, slot):
        return pltpu.make_async_remote_copy(
            src_ref=source.at[ahead(d)],
            dst_ref=target.at[slot],
            send_sem=send.at[d - 1],
            recv_sem=recv.at[d - 1],
            device_id={"resp": ahead(d)},
            device_id_type=MESH,
        )

    for d in range(1, head_devices):
        head_copy(d, mine).start()
    total = parts_ref[mine].astype(jnp.float32)
    for d in range(1, head_devices):
        source = lax.rem(mine + head_devices - d, head_devices)
        head_copy(d, source).wait_recv()
        total = total + head_in[source].astype(jnp.float32)
    for r in range(resp_per):
        for i in range(devices):
            out_rows[i, r * piece : (r + 1) * piece, :] = total[r, i * piece : (i + 1) * piece]
    for d in range(1, devices):
        spread(out_rows, in_rows, row_send, row_recv, d, me).start()
    in_rows[me] = out_rows[me]
    for r in range(resp_per):
        own_ref[r * tokens : (r + 1) * tokens, :] = total[r, prompt_rows:]
    for d in range(1, devices):
        spread(out_rows, in_rows, row_send, row_recv, d, behind(d)).wait_recv()
    slot_at = lax.broadcasted_iota(jnp.int32, (devices, devices), 0)
    for p in range(piece):
        summed = jnp.zeros((devices, share), jnp.float32)
        for r in range(resp_per):
            table = (slot_at == slots[r : r + 1, :]).astype(jnp.float32)
            summed = summed + lax.dot_general(
                table,
                in_rows[:, r * piece + p, :],
                NN,
                precision=lax.Precision.HIGHEST,
                preferred_element_type=jnp.float32,
            )
        out_sums[:, p, :] = summed
    for d in range(1, devices):
        spread(out_sums, in_sums, sum_send, sum_recv, d, me).start()
    in_sums[me] = out_sums[me]
    for d in range(1, devices):
        spread(out_sums, in_sums, sum_send, sum_recv, d, behind(d)).wait_recv()
    for i in range(devices):
        prompt_out[0, i * piece : (i + 1) * piece, :] = in_sums[i]
    for d in range(1, head_devices):
        head_copy(d, mine).wait_send()
    for d in range(1, devices):
        spread(out_rows, in_rows, row_send, row_recv, d, me).wait_send()
        spread(out_sums, in_sums, sum_send, sum_recv, d, me).wait_send()


def finish(parts, slots, resp_devices, prompt_rows):
    head_devices, resp_per, key_count, share = parts.shape
    piece = prompt_rows // resp_devices
    whole = pl.BlockSpec(memory_space=pltpu.VMEM)
    spread = pltpu.SemaphoreType.DMA((resp_devices - 1,))
    across = pltpu.SemaphoreType.DMA((max(head_devices - 1, 1),))
    f32 = jnp.float32
    return pl.pallas_call(
        functools.partial(tail_kernel, resp_devices, head_devices, prompt_rows),
        out_shape=(
            jax.ShapeDtypeStruct((resp_per * (key_count - prompt_rows), share), f32),
            jax.ShapeDtypeStruct((1, prompt_rows, share), f32),
        ),
        in_specs=[whole, whole],
        out_specs=(whole, whole),
        scratch_shapes=[
            pltpu.VMEM(parts.shape, parts.dtype),
            pltpu.VMEM((resp_devices, resp_per * piece, share), f32),
            pltpu.VMEM((resp_devices, resp_per * piece, share), f32),
            pltpu.VMEM((resp_devices, piece, share), f32),
            pltpu.VMEM((resp_devices, piece, share), f32),
            across,
            across,
            spread,
            spread,
            spread,
            spread,
        ],
        compiler_params=pltpu.CompilerParams(collective_id=1, has_side_effects=True),
    )(slots, parts)


def body(
    queries,
    resp_latent,
    prompt_latent,
    up_keys,
    up_values,
    cotangent,
    prompt_len,
    resp_len,
    resp_count,
    owner,
):
    resp_devices = lax.axis_size("resp")
    head_devices = lax.axis_size("head")
    my_index = lax.axis_index("resp")
    resp_total = resp_len.shape[0]
    per_device = resp_total // resp_devices
    row_count = queries.shape[0] // per_device
    prompt_rows = prompt_latent.shape[1]
    latent_cols = prompt_latent.shape[2]
    prompts = jnp.arange(resp_count.shape[0], dtype=jnp.int32)
    earlier = prompts[None, :] < prompts[:, None]
    starts = jnp.sum(jnp.where(earlier, resp_count[None, :], 0), axis=1)
    numbers = jnp.arange(resp_total, dtype=jnp.int32)
    prompt_of = jnp.sum((starts[None, :] <= numbers[:, None]).astype(jnp.int32), axis=1) - 1
    chosen = prompt_of[:, None] == jnp.arange(prompt_len.shape[0], dtype=jnp.int32)[None, :]
    slot_of = jnp.sum(jnp.where(chosen, owner[None, :], 0), axis=1)
    plen_of = jnp.sum(jnp.where(chosen, prompt_len[None, :], 0), axis=1)
    table = jnp.stack([slot_of // 4, (slot_of // 2) % 2, slot_of % 2, plen_of, resp_len], axis=1)
    meta = lax.dynamic_slice_in_dim(table, my_index * per_device, per_device)
    weights = jnp.stack([jnp.swapaxes(up_keys, 1, 2), up_values])
    own_rows = resp_latent.reshape(per_device, row_count, latent_cols)
    attended, grad_query, parts = fused(
        queries, cotangent, weights, prompt_latent, own_rows, meta, resp_devices, head_devices
    )
    slots = slot_of.reshape(resp_devices, per_device).T
    grad_own, at_owner = finish(parts, slots, resp_devices, prompt_rows)
    return attended, grad_query, grad_own, at_owner


def solution(mesh):
    placed = (
        P("resp", "head"),
        P("resp", None),
        P("resp", None, None),
        P("head", None, "resp"),
        P("head", "resp", None),
        P("resp", "head"),
        P(),
        P(),
        P(),
        P(),
    )
    return jax.shard_map(
        body,
        mesh=mesh,
        in_specs=placed,
        out_specs=(
            P("resp", "head"),
            P("resp", "head"),
            P("resp", "head"),
            P("resp", None, "head"),
        ),
        check_vma=False,
    )
```

```python
import functools
import math

import jax
import jax.numpy as jnp
from jax import lax
from jax.experimental import pallas as pl
from jax.experimental.pallas import tpu as pltpu
from jax.sharding import PartitionSpec as P

MESH = pl.DeviceIdType.MESH
NT = (((1,), (1,)), ((), ()))
NN = (((1,), (0,)), ((), ()))
TN = (((0,), (0,)), ((), ()))


def mm(left, right, form):
    return lax.dot_general(left, right, form, preferred_element_type=jnp.float32)


def kernel(
    line,
    chunks,
    heads_per,
    resp_per,
    meta,
    q_ref,
    cot_ref,
    w_ref,
    prompt_ref,
    resp_ref,
    att_ref,
    gq_ref,
    parts_ref,
    gk_ref,
    full,
    prompts,
    keys,
    qf,
    gl,
    lo,
    gf,
    own_sem,
    line_send,
    line_recv,
    pair_send,
    pair_recv,
    lead_send,
    lead_recv,
):
    step = pl.program_id(0)
    ahead = line - 2
    lag = line + 1
    me = lax.axis_index("resp")
    x = lax.rem(me, 2)
    y = lax.rem(lax.div(me, 2), 2)
    z = lax.div(me, 4)

    def at(zz, yy, xx):
        return {"resp": (zz * 2 + yy) * 2 + xx}

    y_peer, x_peer = at(z, 1 - y, x), at(z, y, 1 - x)

    def remote(src, dst, send, recv, peer):
        return pltpu.make_async_remote_copy(
            src_ref=src, dst_ref=dst, send_sem=send, recv_sem=recv, device_id=peer, device_id_type=MESH
        )

    def heads(c):
        return pl.ds(c * heads_per, heads_per)

    def lead(c):
        return pl.ds(c * heads_per, 1)

    def rest(c):
        return pl.ds(c * heads_per + 1, heads_per - 1)

    def own_copy(c):
        return pltpu.make_async_copy(
            w_ref.at[:, heads(c)], full.at[:, z, y, x, heads(c)], own_sem.at[c]
        )

    def line_copy(c, d, source):
        return remote(
            w_ref.at[:, rest(c)],
            full.at[:, source, y, x, rest(c)],
            line_send.at[c, d - 1],
            line_recv.at[c, d - 1],
            at(lax.rem(z + d, line), y, x),
        )

    def pair_copies(c, yy, xx):
        first_k = full.at[0, :, yy[0], xx[0], rest(c)]
        first_v = full.at[1, :, yy[1], xx[1], rest(c)]
        second_k = full.at[0, :, :, xx[2], rest(c)]
        second_v = full.at[1, :, yy[2], :, rest(c)]
        refs = ((first_k, y_peer), (first_v, x_peer), (second_k, x_peer), (second_v, y_peer))
        return [
            remote(ref, ref, pair_send.at[c, i], pair_recv.at[c, i], peer)
            for i, (ref, peer) in enumerate(refs)
        ]

    def out_pairs(c):
        return pair_copies(c, (y, y, y), (x, x, x))

    def in_pairs(c):
        return pair_copies(c, (1 - y, y, 1 - y), (x, 1 - x, 1 - x))

    def lead_x(c, xx):
        ref = full.at[:, z, y, xx, lead(c)]
        return remote(w_ref.at[:, lead(c)], ref, lead_send.at[c, 0], lead_recv.at[c, 0], x_peer)

    def lead_y(c, yy):
        ref = full.at[:, z, yy, :, lead(c)]
        return remote(ref, ref, lead_send.at[c, 1], lead_recv.at[c, 1], y_peer)

    def lead_up(c, j, source):
        ref = full.at[:, source, :, :, lead(c)]
        k = 2 * j
        return remote(ref, ref, lead_send.at[c, k], lead_recv.at[c, k], at(z + 1, y, x))

    def lead_down(c, j, source):
        ref = full.at[:, source, :, :, lead(c)]
        k = 2 * j + 1
        return remote(ref, ref, lead_send.at[c, k], lead_recv.at[c, k], at(z - 1, y, x))

    def lead_arrived(c, j):
        @pl.when(z >= j)
        def _():
            lead_up(c, j, z - j).wait_recv()

        @pl.when(z + j < line)
        def _():
            lead_down(c, j, z + j).wait_recv()

    def lead_onward(c, j, act):
        @pl.when((z + 1 >= j) & (z + 1 < line))
        def _():
            act(lead_up(c, j, z - j + 1))

        @pl.when((z >= 1) & (z + j - 1 < line))
        def _():
            act(lead_down(c, j, z + j - 1))

    def own_prompt():
        return pltpu.make_async_copy(prompt_ref.at[0], prompts.at[z, y, x], own_sem.at[chunks])

    def line_prompt(d, source):
        return remote(
            prompt_ref.at[0],
            prompts.at[source, y, x],
            line_send.at[chunks, d - 1],
            line_recv.at[chunks, d - 1],
            at(lax.rem(z + d, line), y, x),
        )

    def prompt_pairs(yy, xx):
        refs = ((prompts.at[:, yy, x], y_peer), (prompts.at[:, :, xx], x_peer))
        return [
            remote(ref, ref, pair_send.at[chunks, i], pair_recv.at[chunks, i], peer)
            for i, (ref, peer) in enumerate(refs)
        ]

    @pl.when(step == 0)
    def _():
        barrier = pltpu.get_barrier_semaphore()
        for d in range(1, line):
            pl.semaphore_signal(
                barrier, inc=1, device_id=at(lax.rem(z + d, line), y, x), device_id_type=MESH
            )
        pl.semaphore_signal(barrier, inc=1, device_id=y_peer, device_id_type=MESH)
        pl.semaphore_signal(barrier, inc=1, device_id=x_peer, device_id_type=MESH)
        pl.semaphore_wait(barrier, line + 1)
        own_prompt().start()
        for d in range(1, line):
            line_prompt(d, z).start()
        gk_ref[...] = jnp.zeros_like(gk_ref)

    def during(delay):
        return pl.when((step >= delay) & (step < chunks + delay))

    @during(0)
    def _():
        own_copy(step).start()
        lead_x(step, x).start()

    @during(ahead)
    def _():
        c = step - ahead
        for d in range(1, line):
            line_copy(c, d, z).start()

    @during(1)
    def _():
        c = step - 1
        own_copy(c).wait()
        lead_x(c, 1 - x).wait_recv()
        lead_y(c, y).start()

    @during(2)
    def _():
        c = step - 2
        lead_y(c, 1 - y).wait_recv()
        lead_onward(c, 1, lambda copy: copy.start())

    for hop in range(2, line):

        @during(1 + hop)
        def _(hop=hop):
            c = step - 1 - hop
            lead_arrived(c, hop - 1)
            lead_onward(c, hop, lambda copy: copy.start())

    @pl.when(step == 1)
    def _():
        own_prompt().wait()
        for d in range(1, line):
            line_prompt(d, lax.rem(z + line - d, line)).wait_recv()
        prompt_pairs(y, x)[0].start()

    @during(ahead + 1)
    def _():
        c = step - ahead - 1
        for d in range(1, line):
            line_copy(c, d, lax.rem(z + line - d, line)).wait_recv()
        sends = out_pairs(c)
        sends[0].start()
        sends[1].start()

    @pl.when(step == 2)
    def _():
        prompt_pairs(1 - y, 1 - x)[0].wait_recv()
        prompt_pairs(y, x)[1].start()

    @during(ahead + 2)
    def _():
        c = step - ahead - 2
        arrivals, sends = in_pairs(c), out_pairs(c)
        arrivals[0].wait_recv()
        arrivals[1].wait_recv()
        sends[2].start()
        sends[3].start()

    plen_rows = prompt_ref.shape[1]
    tokens = resp_ref.shape[1]
    key_count, key_cols = keys.shape[1], keys.shape[2]
    latent = gl.shape[2]
    slice_cols, nope = w_ref.shape[2], w_ref.shape[3]
    value_cols = nope
    q_cols = q_ref.shape[1] // heads_per
    rows = heads_per * tokens
    scale = 1.0 / math.sqrt(q_cols)

    @pl.when(step == lag)
    def _():
        prompt_pairs(1 - y, 1 - x)[1].wait_recv()
        for r in range(resp_per):
            keys[r, :plen_rows, :] = prompts[meta[r, 0], meta[r, 1], meta[r, 2]]
            keys[r, plen_rows:, :] = resp_ref[r]

    @pl.when(step >= lag)
    def _():
        c = step - lag
        lead_arrived(c, line - 1)
        arrivals = in_pairs(c)
        arrivals[2].wait_recv()
        arrivals[3].wait_recv()

        def weight(kind, h):
            got = full[kind, :, :, :, c * heads_per + h]
            if slice_cols % 16:
                return got.astype(jnp.float32).reshape(latent, nope).astype(jnp.bfloat16)
            return got.reshape(latent, nope)

        token_row = lax.broadcasted_iota(jnp.int32, (resp_per * tokens, 1), 0)
        live = jnp.zeros((resp_per * tokens, 1), jnp.float32)
        for r in range(resp_per):
            inside = (token_row >= r * tokens) & (token_row < r * tokens + meta[r, 4])
            live = jnp.where(inside, 1.0, live)

        for h in range(heads_per):
            wk, wv = weight(0, h), weight(1, h)
            q_latent = mm(q_ref[:, h * q_cols : h * q_cols + nope], wk, NT).astype(jnp.bfloat16)
            rope = q_ref[:, h * q_cols + nope : (h + 1) * q_cols]
            grad_latent = mm(cot_ref[:, h * value_cols : (h + 1) * value_cols], wv, NT) * live
            grad_latent = grad_latent.astype(jnp.bfloat16)
            for r in range(resp_per):
                mine = slice(r * tokens, (r + 1) * tokens)
                place = slice(h * tokens, (h + 1) * tokens)
                qf[r, place, :latent] = q_latent[mine]
                qf[r, place, latent:] = rope[mine]
                gl[r, place, :] = grad_latent[mine]

        key_at = lax.broadcasted_iota(jnp.int32, (key_count, rows), 0)
        token_at = lax.rem(lax.broadcasted_iota(jnp.int32, (key_count, rows), 1), tokens)
        for r in range(resp_per):
            key = keys[r]
            value = key[:, :latent]
            query, grad_latent = qf[r], gl[r]
            scores = mm(key, query, NT) * scale
            last = jnp.where(key_at < plen_rows, meta[r, 3] - 1, token_at + plen_rows)
            scores = jnp.where(key_at <= last, scores, -jnp.inf)
            expo = jnp.exp(scores - jnp.max(scores, axis=0, keepdims=True))
            weights = expo / jnp.sum(expo, axis=0, keepdims=True)
            weights_bf = weights.astype(jnp.bfloat16)
            grad_weights = mm(value, grad_latent, NT)
            inner = jnp.sum(weights * grad_weights, axis=0, keepdims=True)
            grad_scores = (weights * (grad_weights - inner) * scale).astype(jnp.bfloat16)
            lo_r = mm(weights_bf, value, TN).astype(jnp.bfloat16)
            gf_r = mm(grad_scores, key, TN).astype(jnp.bfloat16)
            for h in range(heads_per):
                mine = slice(r * tokens, (r + 1) * tokens)
                place = slice(h * tokens, (h + 1) * tokens)
                lo[h, mine, :] = lo_r[place]
                gf[h, mine, :] = gf_r[place]
            gk_ref[r] += mm(grad_scores, query, NN)
            gk_ref[r, :, :latent] += mm(weights_bf, grad_latent, NN)

        for h in range(heads_per):
            wk, wv = weight(0, h), weight(1, h)
            attended = mm(lo[h], wv, NN) * live
            att_ref[:, h * value_cols : (h + 1) * value_cols] = attended.astype(jnp.bfloat16)
            grad_nope = mm(gf[h, :, :latent], wk, NN).astype(jnp.bfloat16)
            gq_ref[:, h * q_cols : h * q_cols + nope] = grad_nope
            gq_ref[:, h * q_cols + nope : (h + 1) * q_cols] = gf[h, :, latent:]

        sends = out_pairs(c)
        for i in range(4):
            sends[i].wait_send()
        for d in range(1, line):
            line_copy(c, d, z).wait_send()
        lead_x(c, x).wait_send()
        lead_y(c, y).wait_send()
        for hop in range(1, line):
            lead_onward(c, hop, lambda copy: copy.wait_send())

    @pl.when(step == chunks + lag - 1)
    def _():
        share = parts_ref.shape[3]
        for r in range(resp_per):
            for part in range(parts_ref.shape[0]):
                cut = gk_ref[r, :, part * share : (part + 1) * share]
                parts_ref[part, r] = cut.astype(jnp.bfloat16)

    @pl.when(step == lag)
    def _():
        sends = prompt_pairs(y, x)
        sends[0].wait_send()
        sends[1].wait_send()
        for d in range(1, line):
            line_prompt(d, z).wait_send()


def fused(queries, cotangent, weights, prompt_latent, own_rows, meta, resp_devices, head_devices):
    line = resp_devices // 4
    head_count, slice_cols, nope = weights.shape[1:]
    resp_per, tokens, key_cols = own_rows.shape
    prompt_rows = prompt_latent.shape[1]
    heads_per = math.gcd(4, head_count)
    chunks = head_count // heads_per
    row_count = queries.shape[0]
    q_cols = queries.shape[1] // head_count
    latent = slice_cols * resp_devices
    key_count = prompt_rows + tokens
    rows = heads_per * tokens
    bf = jnp.bfloat16

    def tile(t):
        return (0, lax.max(t - line - 1, 0))

    whole = pl.BlockSpec(memory_space=pltpu.VMEM)
    return pl.pallas_call(
        functools.partial(kernel, line, chunks, heads_per, resp_per),
        out_shape=(
            jax.ShapeDtypeStruct(cotangent.shape, bf),
            jax.ShapeDtypeStruct(queries.shape, bf),
            jax.ShapeDtypeStruct(
                (head_devices, resp_per, key_count, key_cols // head_devices), bf
            ),
        ),
        grid=(chunks + line + 1,),
        in_specs=[
            pl.BlockSpec(memory_space=pltpu.SMEM),
            pl.BlockSpec((row_count, heads_per * q_cols), tile),
            pl.BlockSpec((row_count, heads_per * nope), tile),
            whole,
            whole,
            whole,
        ],
        out_specs=(
            pl.BlockSpec((row_count, heads_per * nope), tile),
            pl.BlockSpec((row_count, heads_per * q_cols), tile),
            whole,
        ),
        scratch_shapes=[
            pltpu.VMEM((resp_per, key_count, key_cols), jnp.float32),
            pltpu.VMEM((2, line, 2, 2, head_count, slice_cols, nope), bf),
            pltpu.VMEM((line, 2, 2, prompt_rows, key_cols), bf),
            pltpu.VMEM((resp_per, key_count, key_cols), bf),
            pltpu.VMEM((resp_per, rows, key_cols), bf),
            pltpu.VMEM((resp_per, rows, latent), bf),
            pltpu.VMEM((heads_per, resp_per * tokens, latent), bf),
            pltpu.VMEM((heads_per, resp_per * tokens, key_cols), bf),
            pltpu.SemaphoreType.DMA((chunks + 1,)),
            pltpu.SemaphoreType.DMA((chunks + 1, line - 1)),
            pltpu.SemaphoreType.DMA((chunks + 1, line - 1)),
            pltpu.SemaphoreType.DMA((chunks + 1, 4)),
            pltpu.SemaphoreType.DMA((chunks + 1, 4)),
            pltpu.SemaphoreType.DMA((chunks, 2 * line)),
            pltpu.SemaphoreType.DMA((chunks, 2 * line)),
        ],
        compiler_params=pltpu.CompilerParams(
            collective_id=0, has_side_effects=True, dimension_semantics=("arbitrary",)
        ),
    )(meta, queries, cotangent, weights, prompt_latent, own_rows)


def tail_kernel(
    devices,
    head_devices,
    prompt_rows,
    slots,
    parts_ref,
    own_ref,
    prompt_out,
    head_in,
    out_rows,
    in_rows,
    out_sums,
    in_sums,
    head_send,
    head_recv,
    row_send,
    row_recv,
    sum_send,
    sum_recv,
):
    me = lax.axis_index("resp")
    mine = lax.axis_index("head")
    resp_per, key_count, share = parts_ref.shape[1:]
    tokens = key_count - prompt_rows
    piece = prompt_rows // devices

    def ahead(d):
        return lax.rem(me + d, devices)

    def behind(d):
        return lax.rem(me + devices - d, devices)

    barrier = pltpu.get_barrier_semaphore()
    for d in range(1, devices):
        pl.semaphore_signal(barrier, inc=1, device_id={"resp": ahead(d)}, device_id_type=MESH)
    for d in range(1, head_devices):
        peer = lax.rem(mine + d, head_devices)
        pl.semaphore_signal(barrier, inc=1, device_id={"head": peer}, device_id_type=MESH)
    pl.semaphore_wait(barrier, devices + head_devices - 2)

    def head_copy(d, slot):
        peer = lax.rem(mine + d, head_devices)
        return pltpu.make_async_remote_copy(
            src_ref=parts_ref.at[peer],
            dst_ref=head_in.at[slot],
            send_sem=head_send.at[d - 1],
            recv_sem=head_recv.at[d - 1],
            device_id={"head": peer},
            device_id_type=MESH,
        )

    def spread(source, target, send, recv, d, slot):
        return pltpu.make_async_remote_copy(
            src_ref=source.at[ahead(d)],
            dst_ref=target.at[slot],
            send_sem=send.at[d - 1],
            recv_sem=recv.at[d - 1],
            device_id={"resp": ahead(d)},
            device_id_type=MESH,
        )

    for d in range(1, head_devices):
        head_copy(d, mine).start()
    total = parts_ref[mine].astype(jnp.float32)
    for d in range(1, head_devices):
        source = lax.rem(mine + head_devices - d, head_devices)
        head_copy(d, source).wait_recv()
        total = total + head_in[source].astype(jnp.float32)
    for r in range(resp_per):
        for i in range(devices):
            out_rows[i, r * piece : (r + 1) * piece, :] = total[r, i * piece : (i + 1) * piece]
    for d in range(1, devices):
        spread(out_rows, in_rows, row_send, row_recv, d, me).start()
    in_rows[me] = out_rows[me]
    for r in range(resp_per):
        own_ref[r * tokens : (r + 1) * tokens, :] = total[r, prompt_rows:]
    for d in range(1, devices):
        spread(out_rows, in_rows, row_send, row_recv, d, behind(d)).wait_recv()
    slot_at = lax.broadcasted_iota(jnp.int32, (devices, devices), 0)
    for p in range(piece):
        summed = jnp.zeros((devices, share), jnp.float32)
        for r in range(resp_per):
            table = (slot_at == slots[r : r + 1, :]).astype(jnp.float32)
            summed = summed + lax.dot_general(
                table,
                in_rows[:, r * piece + p, :],
                NN,
                precision=lax.Precision.HIGHEST,
                preferred_element_type=jnp.float32,
            )
        out_sums[:, p, :] = summed
    for d in range(1, devices):
        spread(out_sums, in_sums, sum_send, sum_recv, d, me).start()
    in_sums[me] = out_sums[me]
    for d in range(1, devices):
        spread(out_sums, in_sums, sum_send, sum_recv, d, behind(d)).wait_recv()
    for i in range(devices):
        prompt_out[0, i * piece : (i + 1) * piece, :] = in_sums[i]
    for d in range(1, head_devices):
        head_copy(d, mine).wait_send()
    for d in range(1, devices):
        spread(out_rows, in_rows, row_send, row_recv, d, me).wait_send()
        spread(out_sums, in_sums, sum_send, sum_recv, d, me).wait_send()


def finish(parts, slots, resp_devices, prompt_rows):
    head_devices, resp_per, key_count, share = parts.shape
    piece = prompt_rows // resp_devices
    whole = pl.BlockSpec(memory_space=pltpu.VMEM)
    spread = pltpu.SemaphoreType.DMA((resp_devices - 1,))
    across = pltpu.SemaphoreType.DMA((max(head_devices - 1, 1),))
    f32 = jnp.float32
    return pl.pallas_call(
        functools.partial(tail_kernel, resp_devices, head_devices, prompt_rows),
        out_shape=(
            jax.ShapeDtypeStruct((resp_per * (key_count - prompt_rows), share), f32),
            jax.ShapeDtypeStruct((1, prompt_rows, share), f32),
        ),
        in_specs=[whole, whole],
        out_specs=(whole, whole),
        scratch_shapes=[
            pltpu.VMEM(parts.shape, parts.dtype),
            pltpu.VMEM((resp_devices, resp_per * piece, share), f32),
            pltpu.VMEM((resp_devices, resp_per * piece, share), f32),
            pltpu.VMEM((resp_devices, piece, share), f32),
            pltpu.VMEM((resp_devices, piece, share), f32),
            across,
            across,
            spread,
            spread,
            spread,
            spread,
        ],
        compiler_params=pltpu.CompilerParams(collective_id=1, has_side_effects=True),
    )(slots, parts)


def body(
    queries,
    resp_latent,
    prompt_latent,
    up_keys,
    up_values,
    cotangent,
    prompt_len,
    resp_len,
    resp_count,
    owner,
):
    resp_devices = lax.axis_size("resp")
    head_devices = lax.axis_size("head")
    my_index = lax.axis_index("resp")
    resp_total = resp_len.shape[0]
    per_device = resp_total // resp_devices
    row_count = queries.shape[0] // per_device
    prompt_rows = prompt_latent.shape[1]
    latent_cols = prompt_latent.shape[2]
    prompts = jnp.arange(resp_count.shape[0], dtype=jnp.int32)
    earlier = prompts[None, :] < prompts[:, None]
    starts = jnp.sum(jnp.where(earlier, resp_count[None, :], 0), axis=1)
    numbers = jnp.arange(resp_total, dtype=jnp.int32)
    prompt_of = jnp.sum((starts[None, :] <= numbers[:, None]).astype(jnp.int32), axis=1) - 1
    chosen = prompt_of[:, None] == jnp.arange(prompt_len.shape[0], dtype=jnp.int32)[None, :]
    slot_of = jnp.sum(jnp.where(chosen, owner[None, :], 0), axis=1)
    plen_of = jnp.sum(jnp.where(chosen, prompt_len[None, :], 0), axis=1)
    table = jnp.stack([slot_of // 4, (slot_of // 2) % 2, slot_of % 2, plen_of, resp_len], axis=1)
    meta = lax.dynamic_slice_in_dim(table, my_index * per_device, per_device)
    weights = jnp.stack([jnp.swapaxes(up_keys, 1, 2), up_values])
    own_rows = resp_latent.reshape(per_device, row_count, latent_cols)
    attended, grad_query, parts = fused(
        queries, cotangent, weights, prompt_latent, own_rows, meta, resp_devices, head_devices
    )
    slots = slot_of.reshape(resp_devices, per_device).T
    grad_own, at_owner = finish(parts, slots, resp_devices, prompt_rows)
    return attended, grad_query, grad_own, at_owner


def solution(mesh):
    placed = (
        P("resp", "head"),
        P("resp", None),
        P("resp", None, None),
        P("head", None, "resp"),
        P("head", "resp", None),
        P("resp", "head"),
        P(),
        P(),
        P(),
        P(),
    )
    return jax.shard_map(
        body,
        mesh=mesh,
        in_specs=placed,
        out_specs=(
            P("resp", "head"),
            P("resp", "head"),
            P("resp", "head"),
            P("resp", None, "head"),
        ),
        check_vma=False,
    )
```

```python
import functools
import math

import jax
import jax.numpy as jnp
from jax import lax
from jax.experimental import pallas as pl
from jax.experimental.pallas import tpu as pltpu
from jax.sharding import PartitionSpec as P

MESH = pl.DeviceIdType.MESH
NT = (((1,), (1,)), ((), ()))
NN = (((1,), (0,)), ((), ()))
TN = (((0,), (0,)), ((), ()))


def mm(left, right, form):
    return lax.dot_general(left, right, form, preferred_element_type=jnp.float32)


def kernel(
    line,
    chunks,
    heads_per,
    resp_per,
    meta,
    q_ref,
    cot_ref,
    wk_ref,
    wv_ref,
    prompt_ref,
    resp_ref,
    att_ref,
    gq_ref,
    parts_ref,
    gk_ref,
    full,
    prompts,
    keys,
    qf,
    gl,
    lo,
    gf,
    own_sem,
    line_send,
    line_recv,
    pair_send,
    pair_recv,
    lead_send,
    lead_recv,
):
    step = pl.program_id(0)
    ahead = max(line - 3, 0)
    leads = chunks - chunks // 8
    lag = line + 1
    me = lax.axis_index("resp")
    x = lax.rem(me, 2)
    y = lax.rem(lax.div(me, 2), 2)
    z = lax.div(me, 4)

    def at(zz, yy, xx):
        return {"resp": (zz * 2 + yy) * 2 + xx}

    y_peer, x_peer = at(z, 1 - y, x), at(z, y, 1 - x)

    def remote(src, dst, send, recv, peer):
        return pltpu.make_async_remote_copy(
            src_ref=src, dst_ref=dst, send_sem=send, recv_sem=recv, device_id=peer, device_id_type=MESH
        )

    def heads(c):
        return pl.ds(c * heads_per, heads_per)

    def lead(c):
        return pl.ds(c * heads_per, 1)

    def rest(c):
        return pl.ds(c * heads_per + 1, heads_per - 1)

    def own_copies():
        return [
            pltpu.make_async_copy(ref, full.at[kind, z, y, x], own_sem.at[kind])
            for kind, ref in enumerate((wk_ref, wv_ref))
        ]

    def line_copy(c, d, source, span):
        return remote(
            full.at[:, z, y, x, span],
            full.at[:, source, y, x, span],
            line_send.at[c, d - 1],
            line_recv.at[c, d - 1],
            at(lax.rem(z + d, line), y, x),
        )

    def pair_copies(c, yy, xx, span):
        first_k = full.at[0, :, yy[0], xx[0], span]
        first_v = full.at[1, :, yy[1], xx[1], span]
        second_k = full.at[0, :, :, xx[2], span]
        second_v = full.at[1, :, yy[2], :, span]
        refs = ((first_k, y_peer), (first_v, x_peer), (second_k, x_peer), (second_v, y_peer))
        return [
            remote(ref, ref, pair_send.at[c, i], pair_recv.at[c, i], peer)
            for i, (ref, peer) in enumerate(refs)
        ]

    def out_pairs(c, span):
        return pair_copies(c, (y, y, y), (x, x, x), span)

    def in_pairs(c, span):
        return pair_copies(c, (1 - y, y, 1 - y), (x, 1 - x, 1 - x), span)

    def lead_x(c, xx):
        ref = full.at[:, z, y, xx, lead(c)]
        own = full.at[:, z, y, x, lead(c)]
        return remote(own, ref, lead_send.at[c, 0], lead_recv.at[c, 0], x_peer)

    def lead_y(c, yy):
        ref = full.at[:, z, yy, :, lead(c)]
        return remote(ref, ref, lead_send.at[c, 1], lead_recv.at[c, 1], y_peer)

    def lead_up(c, j, source):
        ref = full.at[:, source, :, :, lead(c)]
        k = 2 * j
        return remote(ref, ref, lead_send.at[c, k], lead_recv.at[c, k], at(z + 1, y, x))

    def lead_down(c, j, source):
        ref = full.at[:, source, :, :, lead(c)]
        k = 2 * j + 1
        return remote(ref, ref, lead_send.at[c, k], lead_recv.at[c, k], at(z - 1, y, x))

    def lead_arrived(c, j):
        @pl.when(z >= j)
        def _():
            lead_up(c, j, z - j).wait_recv()

        @pl.when(z + j < line)
        def _():
            lead_down(c, j, z + j).wait_recv()

    def lead_onward(c, j, act):
        @pl.when((z + 1 >= j) & (z + 1 < line))
        def _():
            act(lead_up(c, j, z - j + 1))

        @pl.when((z >= 1) & (z + j - 1 < line))
        def _():
            act(lead_down(c, j, z + j - 1))

    def own_prompt():
        return pltpu.make_async_copy(prompt_ref.at[0], prompts.at[z, y, x], own_sem.at[2])

    def line_prompt(d, source):
        return remote(
            prompt_ref.at[0],
            prompts.at[source, y, x],
            line_send.at[chunks, d - 1],
            line_recv.at[chunks, d - 1],
            at(lax.rem(z + d, line), y, x),
        )

    def prompt_pairs(yy, xx):
        refs = ((prompts.at[:, yy, x], y_peer), (prompts.at[:, :, xx], x_peer))
        return [
            remote(ref, ref, pair_send.at[chunks, i], pair_recv.at[chunks, i], peer)
            for i, (ref, peer) in enumerate(refs)
        ]

    @pl.when(step == 0)
    def _():
        for copy in own_copies():
            copy.start()
        barrier = pltpu.get_barrier_semaphore()
        for d in range(1, line):
            pl.semaphore_signal(
                barrier, inc=1, device_id=at(lax.rem(z + d, line), y, x), device_id_type=MESH
            )
        pl.semaphore_signal(barrier, inc=1, device_id=y_peer, device_id_type=MESH)
        pl.semaphore_signal(barrier, inc=1, device_id=x_peer, device_id_type=MESH)
        pl.semaphore_wait(barrier, line + 1)
        own_prompt().start()
        for d in range(1, line):
            line_prompt(d, z).start()
        gk_ref[...] = jnp.zeros_like(gk_ref)
        for copy in own_copies():
            copy.wait()

    def during(delay, count):
        return pl.when((step >= delay) & (step < count + delay))

    def spanned(c, act):
        @pl.when(c < leads)
        def _():
            act(rest(c))

        @pl.when(c >= leads)
        def _():
            act(heads(c))

    @during(0, leads)
    def _():
        lead_x(step, x).start()

    @during(ahead, chunks)
    def _():
        c = step - ahead

        def act(span):
            for d in range(1, line):
                line_copy(c, d, z, span).start()

        spanned(c, act)

    @during(1, leads)
    def _():
        c = step - 1
        lead_x(c, 1 - x).wait_recv()
        lead_y(c, y).start()

    @during(2, leads)
    def _():
        c = step - 2
        lead_y(c, 1 - y).wait_recv()
        lead_onward(c, 1, lambda copy: copy.start())

    for hop in range(2, line):

        @during(1 + hop, leads)
        def _(hop=hop):
            c = step - 1 - hop
            lead_arrived(c, hop - 1)
            lead_onward(c, hop, lambda copy: copy.start())

    @pl.when(step == 1)
    def _():
        own_prompt().wait()
        for d in range(1, line):
            line_prompt(d, lax.rem(z + line - d, line)).wait_recv()
        prompt_pairs(y, x)[0].start()

    @during(ahead + 1, chunks)
    def _():
        c = step - ahead - 1

        def act(span):
            for d in range(1, line):
                line_copy(c, d, lax.rem(z + line - d, line), span).wait_recv()
            sends = out_pairs(c, span)
            sends[0].start()
            sends[1].start()

        spanned(c, act)

    @pl.when(step == 2)
    def _():
        prompt_pairs(1 - y, 1 - x)[0].wait_recv()
        prompt_pairs(y, x)[1].start()

    @during(ahead + 2, chunks)
    def _():
        c = step - ahead - 2

        def act(span):
            arrivals, sends = in_pairs(c, span), out_pairs(c, span)
            arrivals[0].wait_recv()
            arrivals[1].wait_recv()
            sends[2].start()
            sends[3].start()

        spanned(c, act)

    plen_rows = prompt_ref.shape[1]
    tokens = resp_ref.shape[1]
    key_count, key_cols = keys.shape[1], keys.shape[2]
    latent = gl.shape[2]
    slice_cols, nope = wk_ref.shape[1], wk_ref.shape[2]
    value_cols = nope
    q_cols = q_ref.shape[1] // heads_per
    rows = heads_per * tokens
    scale = 1.0 / math.sqrt(q_cols)

    @pl.when(step == lag)
    def _():
        prompt_pairs(1 - y, 1 - x)[1].wait_recv()
        for r in range(resp_per):
            keys[r, :plen_rows, :] = prompts[meta[r, 0], meta[r, 1], meta[r, 2]]
            keys[r, plen_rows:, :] = resp_ref[r]

    @pl.when(step >= lag)
    def _():
        c = step - lag

        @pl.when(c < leads)
        def _():
            lead_arrived(c, line - 1)

        def arrive(span):
            arrivals = in_pairs(c, span)
            arrivals[2].wait_recv()
            arrivals[3].wait_recv()

        spanned(c, arrive)

        def weight(kind, h):
            got = full[kind, :, :, :, c * heads_per + h]
            if slice_cols % 16:
                return got.astype(jnp.float32).reshape(latent, nope).astype(jnp.bfloat16)
            return got.reshape(latent, nope)

        token_row = lax.broadcasted_iota(jnp.int32, (resp_per * tokens, 1), 0)
        live = jnp.zeros((resp_per * tokens, 1), jnp.float32)
        for r in range(resp_per):
            inside = (token_row >= r * tokens) & (token_row < r * tokens + meta[r, 4])
            live = jnp.where(inside, 1.0, live)

        for h in range(heads_per):
            wk, wv = weight(0, h), weight(1, h)
            q_latent = mm(q_ref[:, h * q_cols : h * q_cols + nope], wk, NT).astype(jnp.bfloat16)
            rope = q_ref[:, h * q_cols + nope : (h + 1) * q_cols]
            grad_latent = mm(cot_ref[:, h * value_cols : (h + 1) * value_cols], wv, NT) * live
            grad_latent = grad_latent.astype(jnp.bfloat16)
            for r in range(resp_per):
                mine = slice(r * tokens, (r + 1) * tokens)
                place = slice(h * tokens, (h + 1) * tokens)
                qf[r, place, :latent] = q_latent[mine]
                qf[r, place, latent:] = rope[mine]
                gl[r, place, :] = grad_latent[mine]

        key_at = lax.broadcasted_iota(jnp.int32, (key_count, rows), 0)
        token_at = lax.rem(lax.broadcasted_iota(jnp.int32, (key_count, rows), 1), tokens)
        for r in range(resp_per):
            key = keys[r]
            value = key[:, :latent]
            query, grad_latent = qf[r], gl[r]
            scores = mm(key, query, NT) * scale
            last = jnp.where(key_at < plen_rows, meta[r, 3] - 1, token_at + plen_rows)
            scores = jnp.where(key_at <= last, scores, -jnp.inf)
            expo = jnp.exp(scores - jnp.max(scores, axis=0, keepdims=True))
            weights = expo / jnp.sum(expo, axis=0, keepdims=True)
            weights_bf = weights.astype(jnp.bfloat16)
            grad_weights = mm(value, grad_latent, NT)
            inner = jnp.sum(weights * grad_weights, axis=0, keepdims=True)
            grad_scores = (weights * (grad_weights - inner) * scale).astype(jnp.bfloat16)
            lo_r = mm(weights_bf, value, TN).astype(jnp.bfloat16)
            gf_r = mm(grad_scores, key, TN).astype(jnp.bfloat16)
            for h in range(heads_per):
                mine = slice(r * tokens, (r + 1) * tokens)
                place = slice(h * tokens, (h + 1) * tokens)
                lo[h, mine, :] = lo_r[place]
                gf[h, mine, :] = gf_r[place]
            gk_ref[r] += mm(grad_scores, query, NN)
            gk_ref[r, :, :latent] += mm(weights_bf, grad_latent, NN)

        for h in range(heads_per):
            wk, wv = weight(0, h), weight(1, h)
            attended = mm(lo[h], wv, NN) * live
            att_ref[:, h * value_cols : (h + 1) * value_cols] = attended.astype(jnp.bfloat16)
            grad_nope = mm(gf[h, :, :latent], wk, NN).astype(jnp.bfloat16)
            gq_ref[:, h * q_cols : h * q_cols + nope] = grad_nope
            gq_ref[:, h * q_cols + nope : (h + 1) * q_cols] = gf[h, :, latent:]

        def settle(span):
            sends = out_pairs(c, span)
            for i in range(4):
                sends[i].wait_send()
            for d in range(1, line):
                line_copy(c, d, z, span).wait_send()

        spanned(c, settle)

        @pl.when(c < leads)
        def _():
            lead_x(c, x).wait_send()
            lead_y(c, y).wait_send()
            for hop in range(1, line):
                lead_onward(c, hop, lambda copy: copy.wait_send())

    @pl.when(step == chunks + lag - 1)
    def _():
        share = parts_ref.shape[3]
        for r in range(resp_per):
            for part in range(parts_ref.shape[0]):
                cut = gk_ref[r, :, part * share : (part + 1) * share]
                parts_ref[part, r] = cut.astype(jnp.bfloat16)

    @pl.when(step == lag)
    def _():
        sends = prompt_pairs(y, x)
        sends[0].wait_send()
        sends[1].wait_send()
        for d in range(1, line):
            line_prompt(d, z).wait_send()


def fused(queries, cotangent, wk, wv, prompt_latent, own_rows, meta, resp_devices, head_devices):
    line = resp_devices // 4
    head_count, slice_cols, nope = wk.shape
    resp_per, tokens, key_cols = own_rows.shape
    prompt_rows = prompt_latent.shape[1]
    heads_per = math.gcd(4, head_count)
    chunks = head_count // heads_per
    row_count = queries.shape[0]
    q_cols = queries.shape[1] // head_count
    latent = slice_cols * resp_devices
    key_count = prompt_rows + tokens
    rows = heads_per * tokens
    bf = jnp.bfloat16

    def tile(t):
        return (0, lax.max(t - line - 1, 0))

    whole = pl.BlockSpec(memory_space=pltpu.VMEM)
    return pl.pallas_call(
        functools.partial(kernel, line, chunks, heads_per, resp_per),
        out_shape=(
            jax.ShapeDtypeStruct(cotangent.shape, bf),
            jax.ShapeDtypeStruct(queries.shape, bf),
            jax.ShapeDtypeStruct(
                (head_devices, resp_per, key_count, key_cols // head_devices), bf
            ),
        ),
        grid=(chunks + line + 1,),
        in_specs=[
            pl.BlockSpec(memory_space=pltpu.SMEM),
            pl.BlockSpec((row_count, heads_per * q_cols), tile),
            pl.BlockSpec((row_count, heads_per * nope), tile),
            pl.BlockSpec(memory_space=pl.ANY),
            pl.BlockSpec(memory_space=pl.ANY),
            whole,
            whole,
        ],
        out_specs=(
            pl.BlockSpec((row_count, heads_per * nope), tile),
            pl.BlockSpec((row_count, heads_per * q_cols), tile),
            whole,
        ),
        scratch_shapes=[
            pltpu.VMEM((resp_per, key_count, key_cols), jnp.float32),
            pltpu.VMEM((2, line, 2, 2, head_count, slice_cols, nope), bf),
            pltpu.VMEM((line, 2, 2, prompt_rows, key_cols), bf),
            pltpu.VMEM((resp_per, key_count, key_cols), bf),
            pltpu.VMEM((resp_per, rows, key_cols), bf),
            pltpu.VMEM((resp_per, rows, latent), bf),
            pltpu.VMEM((heads_per, resp_per * tokens, latent), bf),
            pltpu.VMEM((heads_per, resp_per * tokens, key_cols), bf),
            pltpu.SemaphoreType.DMA((3,)),
            pltpu.SemaphoreType.DMA((chunks + 1, line - 1)),
            pltpu.SemaphoreType.DMA((chunks + 1, line - 1)),
            pltpu.SemaphoreType.DMA((chunks + 1, 4)),
            pltpu.SemaphoreType.DMA((chunks + 1, 4)),
            pltpu.SemaphoreType.DMA((chunks, 2 * line)),
            pltpu.SemaphoreType.DMA((chunks, 2 * line)),
        ],
        compiler_params=pltpu.CompilerParams(
            collective_id=0, has_side_effects=True, dimension_semantics=("arbitrary",)
        ),
    )(meta, queries, cotangent, wk, wv, prompt_latent, own_rows)


def tail_kernel(
    devices,
    head_devices,
    prompt_rows,
    slots,
    parts_ref,
    own_ref,
    prompt_out,
    head_in,
    out_rows,
    in_rows,
    out_sums,
    in_sums,
    head_send,
    head_recv,
    row_send,
    row_recv,
    sum_send,
    sum_recv,
):
    me = lax.axis_index("resp")
    mine = lax.axis_index("head")
    resp_per, key_count, share = parts_ref.shape[1:]
    tokens = key_count - prompt_rows
    piece = prompt_rows // devices

    def ahead(d):
        return lax.rem(me + d, devices)

    def behind(d):
        return lax.rem(me + devices - d, devices)

    barrier = pltpu.get_barrier_semaphore()
    for d in range(1, devices):
        pl.semaphore_signal(barrier, inc=1, device_id={"resp": ahead(d)}, device_id_type=MESH)
    for d in range(1, head_devices):
        peer = lax.rem(mine + d, head_devices)
        pl.semaphore_signal(barrier, inc=1, device_id={"head": peer}, device_id_type=MESH)
    pl.semaphore_wait(barrier, devices + head_devices - 2)

    def head_copy(d, slot):
        peer = lax.rem(mine + d, head_devices)
        return pltpu.make_async_remote_copy(
            src_ref=parts_ref.at[peer],
            dst_ref=head_in.at[slot],
            send_sem=head_send.at[d - 1],
            recv_sem=head_recv.at[d - 1],
            device_id={"head": peer},
            device_id_type=MESH,
        )

    def spread(source, target, send, recv, d, slot):
        return pltpu.make_async_remote_copy(
            src_ref=source.at[ahead(d)],
            dst_ref=target.at[slot],
            send_sem=send.at[d - 1],
            recv_sem=recv.at[d - 1],
            device_id={"resp": ahead(d)},
            device_id_type=MESH,
        )

    for d in range(1, head_devices):
        head_copy(d, mine).start()
    total = parts_ref[mine].astype(jnp.float32)
    for d in range(1, head_devices):
        source = lax.rem(mine + head_devices - d, head_devices)
        head_copy(d, source).wait_recv()
        total = total + head_in[source].astype(jnp.float32)
    for r in range(resp_per):
        for i in range(devices):
            out_rows[i, r * piece : (r + 1) * piece, :] = total[r, i * piece : (i + 1) * piece]
    for d in range(1, devices):
        spread(out_rows, in_rows, row_send, row_recv, d, me).start()
    in_rows[me] = out_rows[me]
    for r in range(resp_per):
        own_ref[r * tokens : (r + 1) * tokens, :] = total[r, prompt_rows:]
    for d in range(1, devices):
        spread(out_rows, in_rows, row_send, row_recv, d, behind(d)).wait_recv()
    slot_at = lax.broadcasted_iota(jnp.int32, (devices, devices), 0)
    for p in range(piece):
        summed = jnp.zeros((devices, share), jnp.float32)
        for r in range(resp_per):
            table = (slot_at == slots[r : r + 1, :]).astype(jnp.float32)
            summed = summed + lax.dot_general(
                table,
                in_rows[:, r * piece + p, :],
                NN,
                precision=lax.Precision.HIGHEST,
                preferred_element_type=jnp.float32,
            )
        out_sums[:, p, :] = summed
    for d in range(1, devices):
        spread(out_sums, in_sums, sum_send, sum_recv, d, me).start()
    in_sums[me] = out_sums[me]
    for d in range(1, devices):
        spread(out_sums, in_sums, sum_send, sum_recv, d, behind(d)).wait_recv()
    for i in range(devices):
        prompt_out[0, i * piece : (i + 1) * piece, :] = in_sums[i]
    for d in range(1, head_devices):
        head_copy(d, mine).wait_send()
    for d in range(1, devices):
        spread(out_rows, in_rows, row_send, row_recv, d, me).wait_send()
        spread(out_sums, in_sums, sum_send, sum_recv, d, me).wait_send()


def finish(parts, slots, resp_devices, prompt_rows):
    head_devices, resp_per, key_count, share = parts.shape
    piece = prompt_rows // resp_devices
    whole = pl.BlockSpec(memory_space=pltpu.VMEM)
    spread = pltpu.SemaphoreType.DMA((resp_devices - 1,))
    across = pltpu.SemaphoreType.DMA((max(head_devices - 1, 1),))
    f32 = jnp.float32
    return pl.pallas_call(
        functools.partial(tail_kernel, resp_devices, head_devices, prompt_rows),
        out_shape=(
            jax.ShapeDtypeStruct((resp_per * (key_count - prompt_rows), share), f32),
            jax.ShapeDtypeStruct((1, prompt_rows, share), f32),
        ),
        in_specs=[whole, whole],
        out_specs=(whole, whole),
        scratch_shapes=[
            pltpu.VMEM(parts.shape, parts.dtype),
            pltpu.VMEM((resp_devices, resp_per * piece, share), f32),
            pltpu.VMEM((resp_devices, resp_per * piece, share), f32),
            pltpu.VMEM((resp_devices, piece, share), f32),
            pltpu.VMEM((resp_devices, piece, share), f32),
            across,
            across,
            spread,
            spread,
            spread,
            spread,
        ],
        compiler_params=pltpu.CompilerParams(collective_id=1, has_side_effects=True),
    )(slots, parts)


def body(
    queries,
    resp_latent,
    prompt_latent,
    up_keys,
    up_values,
    cotangent,
    prompt_len,
    resp_len,
    resp_count,
    owner,
):
    resp_devices = lax.axis_size("resp")
    head_devices = lax.axis_size("head")
    my_index = lax.axis_index("resp")
    resp_total = resp_len.shape[0]
    per_device = resp_total // resp_devices
    row_count = queries.shape[0] // per_device
    prompt_rows = prompt_latent.shape[1]
    latent_cols = prompt_latent.shape[2]
    prompts = jnp.arange(resp_count.shape[0], dtype=jnp.int32)
    earlier = prompts[None, :] < prompts[:, None]
    starts = jnp.sum(jnp.where(earlier, resp_count[None, :], 0), axis=1)
    numbers = jnp.arange(resp_total, dtype=jnp.int32)
    prompt_of = jnp.sum((starts[None, :] <= numbers[:, None]).astype(jnp.int32), axis=1) - 1
    chosen = prompt_of[:, None] == jnp.arange(prompt_len.shape[0], dtype=jnp.int32)[None, :]
    slot_of = jnp.sum(jnp.where(chosen, owner[None, :], 0), axis=1)
    plen_of = jnp.sum(jnp.where(chosen, prompt_len[None, :], 0), axis=1)
    table = jnp.stack([slot_of // 4, (slot_of // 2) % 2, slot_of % 2, plen_of, resp_len], axis=1)
    meta = lax.dynamic_slice_in_dim(table, my_index * per_device, per_device)
    keys_t = jnp.swapaxes(up_keys, 1, 2)
    own_rows = resp_latent.reshape(per_device, row_count, latent_cols)
    attended, grad_query, parts = fused(
        queries, cotangent, keys_t, up_values, prompt_latent, own_rows, meta, resp_devices, head_devices
    )
    slots = slot_of.reshape(resp_devices, per_device).T
    grad_own, at_owner = finish(parts, slots, resp_devices, prompt_rows)
    return attended, grad_query, grad_own, at_owner


def solution(mesh):
    placed = (
        P("resp", "head"),
        P("resp", None),
        P("resp", None, None),
        P("head", None, "resp"),
        P("head", "resp", None),
        P("resp", "head"),
        P(),
        P(),
        P(),
        P(),
    )
    return jax.shard_map(
        body,
        mesh=mesh,
        in_specs=placed,
        out_specs=(
            P("resp", "head"),
            P("resp", "head"),
            P("resp", "head"),
            P("resp", None, "head"),
        ),
        check_vma=False,
    )
```

```python
import functools
import math

import jax
import jax.numpy as jnp
from jax import lax
from jax.experimental import pallas as pl
from jax.experimental.pallas import tpu as pltpu
from jax.sharding import PartitionSpec as P

MESH = pl.DeviceIdType.MESH
NT = (((1,), (1,)), ((), ()))
NN = (((1,), (0,)), ((), ()))
TN = (((0,), (0,)), ((), ()))


def mm(left, right, form):
    return lax.dot_general(left, right, form, preferred_element_type=jnp.float32)


def kernel(
    line,
    chunks,
    heads_per,
    resp_per,
    meta,
    q_ref,
    cot_ref,
    wk_ref,
    wv_ref,
    prompt_ref,
    resp_ref,
    att_ref,
    gq_ref,
    parts_ref,
    gk_ref,
    full,
    prompts,
    keys,
    qf,
    gl,
    lo,
    gf,
    own_sem,
    line_send,
    line_recv,
    pair_send,
    pair_recv,
    lead_send,
    lead_recv,
):
    step = pl.program_id(0)
    ahead = line - 2
    leads = chunks
    lag = line + 1
    me = lax.axis_index("resp")
    x = lax.rem(me, 2)
    y = lax.rem(lax.div(me, 2), 2)
    z = lax.div(me, 4)

    def at(zz, yy, xx):
        return {"resp": (zz * 2 + yy) * 2 + xx}

    y_peer, x_peer = at(z, 1 - y, x), at(z, y, 1 - x)

    def remote(src, dst, send, recv, peer):
        return pltpu.make_async_remote_copy(
            src_ref=src, dst_ref=dst, send_sem=send, recv_sem=recv, device_id=peer, device_id_type=MESH
        )

    def heads(c):
        return pl.ds(c * heads_per, heads_per)

    def lead(c):
        return pl.ds(c * heads_per, 1)

    def rest(c):
        return pl.ds(c * heads_per + 1, heads_per - 1)

    def own_copies():
        return [
            pltpu.make_async_copy(ref, full.at[kind, z, y, x], own_sem.at[kind])
            for kind, ref in enumerate((wk_ref, wv_ref))
        ]

    def line_copy(c, d, source, span):
        return remote(
            full.at[:, z, y, x, span],
            full.at[:, source, y, x, span],
            line_send.at[c, d - 1],
            line_recv.at[c, d - 1],
            at(lax.rem(z + d, line), y, x),
        )

    def pair_copies(c, yy, xx, span):
        first_k = full.at[0, :, yy[0], xx[0], span]
        first_v = full.at[1, :, yy[1], xx[1], span]
        second_k = full.at[0, :, :, xx[2], span]
        second_v = full.at[1, :, yy[2], :, span]
        refs = ((first_k, y_peer), (first_v, x_peer), (second_k, x_peer), (second_v, y_peer))
        return [
            remote(ref, ref, pair_send.at[c, i], pair_recv.at[c, i], peer)
            for i, (ref, peer) in enumerate(refs)
        ]

    def out_pairs(c, span):
        return pair_copies(c, (y, y, y), (x, x, x), span)

    def in_pairs(c, span):
        return pair_copies(c, (1 - y, y, 1 - y), (x, 1 - x, 1 - x), span)

    def lead_x(c, xx):
        ref = full.at[:, z, y, xx, lead(c)]
        own = full.at[:, z, y, x, lead(c)]
        return remote(own, ref, lead_send.at[c, 0], lead_recv.at[c, 0], x_peer)

    def lead_y(c, yy):
        ref = full.at[:, z, yy, :, lead(c)]
        return remote(ref, ref, lead_send.at[c, 1], lead_recv.at[c, 1], y_peer)

    def lead_up(c, j, source):
        ref = full.at[:, source, :, :, lead(c)]
        k = 2 * j
        return remote(ref, ref, lead_send.at[c, k], lead_recv.at[c, k], at(z + 1, y, x))

    def lead_down(c, j, source):
        ref = full.at[:, source, :, :, lead(c)]
        k = 2 * j + 1
        return remote(ref, ref, lead_send.at[c, k], lead_recv.at[c, k], at(z - 1, y, x))

    def lead_arrived(c, j):
        @pl.when(z >= j)
        def _():
            lead_up(c, j, z - j).wait_recv()

        @pl.when(z + j < line)
        def _():
            lead_down(c, j, z + j).wait_recv()

    def lead_onward(c, j, act):
        @pl.when((z + 1 >= j) & (z + 1 < line))
        def _():
            act(lead_up(c, j, z - j + 1))

        @pl.when((z >= 1) & (z + j - 1 < line))
        def _():
            act(lead_down(c, j, z + j - 1))

    def own_prompt():
        return pltpu.make_async_copy(prompt_ref.at[0], prompts.at[z, y, x], own_sem.at[2])

    def line_prompt(d, source):
        return remote(
            prompt_ref.at[0],
            prompts.at[source, y, x],
            line_send.at[chunks, d - 1],
            line_recv.at[chunks, d - 1],
            at(lax.rem(z + d, line), y, x),
        )

    def prompt_pairs(yy, xx):
        refs = ((prompts.at[:, yy, x], y_peer), (prompts.at[:, :, xx], x_peer))
        return [
            remote(ref, ref, pair_send.at[chunks, i], pair_recv.at[chunks, i], peer)
            for i, (ref, peer) in enumerate(refs)
        ]

    @pl.when(step == 0)
    def _():
        for copy in own_copies():
            copy.start()
        barrier = pltpu.get_barrier_semaphore()
        for d in range(1, line):
            pl.semaphore_signal(
                barrier, inc=1, device_id=at(lax.rem(z + d, line), y, x), device_id_type=MESH
            )
        pl.semaphore_signal(barrier, inc=1, device_id=y_peer, device_id_type=MESH)
        pl.semaphore_signal(barrier, inc=1, device_id=x_peer, device_id_type=MESH)
        pl.semaphore_wait(barrier, line + 1)
        own_prompt().start()
        for d in range(1, line):
            line_prompt(d, z).start()
        gk_ref[...] = jnp.zeros_like(gk_ref)
        for copy in own_copies():
            copy.wait()

    def during(delay, count):
        return pl.when((step >= delay) & (step < count + delay))

    def spanned(c, act):
        @pl.when(c < leads)
        def _():
            act(rest(c))

        @pl.when(c >= leads)
        def _():
            act(heads(c))

    @during(0, leads)
    def _():
        lead_x(step, x).start()

    @during(ahead, chunks)
    def _():
        c = step - ahead

        def act(span):
            for d in range(1, line):
                line_copy(c, d, z, span).start()

        spanned(c, act)

    @during(1, leads)
    def _():
        c = step - 1
        lead_x(c, 1 - x).wait_recv()
        lead_y(c, y).start()

    @during(2, leads)
    def _():
        c = step - 2
        lead_y(c, 1 - y).wait_recv()
        lead_onward(c, 1, lambda copy: copy.start())

    for hop in range(2, line):

        @during(1 + hop, leads)
        def _(hop=hop):
            c = step - 1 - hop
            lead_arrived(c, hop - 1)
            lead_onward(c, hop, lambda copy: copy.start())

    @pl.when(step == 1)
    def _():
        own_prompt().wait()
        for d in range(1, line):
            line_prompt(d, lax.rem(z + line - d, line)).wait_recv()
        prompt_pairs(y, x)[0].start()

    @during(ahead + 1, chunks)
    def _():
        c = step - ahead - 1

        def act(span):
            for d in range(1, line):
                line_copy(c, d, lax.rem(z + line - d, line), span).wait_recv()
            sends = out_pairs(c, span)
            sends[0].start()
            sends[1].start()

        spanned(c, act)

    @pl.when(step == 2)
    def _():
        prompt_pairs(1 - y, 1 - x)[0].wait_recv()
        prompt_pairs(y, x)[1].start()

    @during(ahead + 2, chunks)
    def _():
        c = step - ahead - 2

        def act(span):
            arrivals, sends = in_pairs(c, span), out_pairs(c, span)
            arrivals[0].wait_recv()
            arrivals[1].wait_recv()
            sends[2].start()
            sends[3].start()

        spanned(c, act)

    plen_rows = prompt_ref.shape[1]
    tokens = resp_ref.shape[1] // resp_per
    key_count, key_cols = keys.shape[1], keys.shape[2]
    latent = gl.shape[2]
    slice_cols, nope = wk_ref.shape[1], wk_ref.shape[2]
    value_cols = nope
    q_cols = q_ref.shape[1] // heads_per
    rows = heads_per * tokens
    scale = 1.0 / math.sqrt(q_cols)

    @pl.when(step == lag)
    def _():
        prompt_pairs(1 - y, 1 - x)[1].wait_recv()
        for r in range(resp_per):
            keys[r, :plen_rows, :] = prompts[meta[r, 0], meta[r, 1], meta[r, 2]]
            own = resp_ref[:, r * tokens : (r + 1) * tokens].astype(jnp.float32)
            keys[r, plen_rows:, :] = jnp.transpose(own).astype(jnp.bfloat16)

    @pl.when(step >= lag)
    def _():
        c = step - lag

        @pl.when(c < leads)
        def _():
            lead_arrived(c, line - 1)

        def arrive(span):
            arrivals = in_pairs(c, span)
            arrivals[2].wait_recv()
            arrivals[3].wait_recv()

        spanned(c, arrive)

        def weight(kind, h):
            got = full[kind, :, :, :, c * heads_per + h]
            if slice_cols % 16:
                return got.astype(jnp.float32).reshape(latent, nope).astype(jnp.bfloat16)
            return got.reshape(latent, nope)

        token_row = lax.broadcasted_iota(jnp.int32, (resp_per * tokens, 1), 0)
        live = jnp.zeros((resp_per * tokens, 1), jnp.float32)
        for r in range(resp_per):
            inside = (token_row >= r * tokens) & (token_row < r * tokens + meta[r, 4])
            live = jnp.where(inside, 1.0, live)

        for h in range(heads_per):
            wk, wv = weight(0, h), weight(1, h)
            q_latent = mm(q_ref[:, h * q_cols : h * q_cols + nope], wk, NT).astype(jnp.bfloat16)
            rope = q_ref[:, h * q_cols + nope : (h + 1) * q_cols]
            grad_latent = mm(cot_ref[:, h * value_cols : (h + 1) * value_cols], wv, NT) * live
            grad_latent = grad_latent.astype(jnp.bfloat16)
            for r in range(resp_per):
                mine = slice(r * tokens, (r + 1) * tokens)
                place = slice(h * tokens, (h + 1) * tokens)
                qf[r, place, :latent] = q_latent[mine]
                qf[r, place, latent:] = rope[mine]
                gl[r, place, :] = grad_latent[mine]

        key_at = lax.broadcasted_iota(jnp.int32, (key_count, rows), 0)
        token_at = lax.rem(lax.broadcasted_iota(jnp.int32, (key_count, rows), 1), tokens)
        for r in range(resp_per):
            key = keys[r]
            value = key[:, :latent]
            query, grad_latent = qf[r], gl[r]
            scores = mm(key, query, NT) * scale
            last = jnp.where(key_at < plen_rows, meta[r, 3] - 1, token_at + plen_rows)
            scores = jnp.where(key_at <= last, scores, -jnp.inf)
            expo = jnp.exp(scores - jnp.max(scores, axis=0, keepdims=True))
            weights = expo / jnp.sum(expo, axis=0, keepdims=True)
            weights_bf = weights.astype(jnp.bfloat16)
            grad_weights = mm(value, grad_latent, NT)
            inner = jnp.sum(weights * grad_weights, axis=0, keepdims=True)
            grad_scores = (weights * (grad_weights - inner) * scale).astype(jnp.bfloat16)
            lo_r = mm(weights_bf, value, TN).astype(jnp.bfloat16)
            gf_r = mm(grad_scores, key, TN).astype(jnp.bfloat16)
            for h in range(heads_per):
                mine = slice(r * tokens, (r + 1) * tokens)
                place = slice(h * tokens, (h + 1) * tokens)
                lo[h, mine, :] = lo_r[place]
                gf[h, mine, :] = gf_r[place]
            gk_ref[r] += mm(grad_scores, query, NN)
            gk_ref[r, :, :latent] += mm(weights_bf, grad_latent, NN)

        for h in range(heads_per):
            wk, wv = weight(0, h), weight(1, h)
            attended = mm(lo[h], wv, NN) * live
            att_ref[:, h * value_cols : (h + 1) * value_cols] = attended.astype(jnp.bfloat16)
            grad_nope = mm(gf[h, :, :latent], wk, NN).astype(jnp.bfloat16)
            gq_ref[:, h * q_cols : h * q_cols + nope] = grad_nope
            gq_ref[:, h * q_cols + nope : (h + 1) * q_cols] = gf[h, :, latent:]

        def settle(span):
            sends = out_pairs(c, span)
            for i in range(4):
                sends[i].wait_send()
            for d in range(1, line):
                line_copy(c, d, z, span).wait_send()

        spanned(c, settle)

        @pl.when(c < leads)
        def _():
            lead_x(c, x).wait_send()
            lead_y(c, y).wait_send()
            for hop in range(1, line):
                lead_onward(c, hop, lambda copy: copy.wait_send())

    @pl.when(step == chunks + lag - 1)
    def _():
        share = parts_ref.shape[3]
        for r in range(resp_per):
            for part in range(parts_ref.shape[0]):
                cut = gk_ref[r, :, part * share : (part + 1) * share]
                parts_ref[part, r] = cut.astype(jnp.bfloat16)

    @pl.when(step == lag)
    def _():
        sends = prompt_pairs(y, x)
        sends[0].wait_send()
        sends[1].wait_send()
        for d in range(1, line):
            line_prompt(d, z).wait_send()


def fused(queries, cotangent, wk, wv, prompt_latent, own_cols, meta, resp_devices, head_devices):
    resp_per = meta.shape[0]
    line = resp_devices // 4
    head_count, slice_cols, nope = wk.shape
    key_cols = own_cols.shape[0]
    tokens = own_cols.shape[1] // resp_per
    prompt_rows = prompt_latent.shape[1]
    heads_per = math.gcd(4, head_count)
    chunks = head_count // heads_per
    row_count = queries.shape[0]
    q_cols = queries.shape[1] // head_count
    latent = slice_cols * resp_devices
    key_count = prompt_rows + tokens
    rows = heads_per * tokens
    bf = jnp.bfloat16

    def tile(t):
        return (0, lax.max(t - line - 1, 0))

    whole = pl.BlockSpec(memory_space=pltpu.VMEM)
    return pl.pallas_call(
        functools.partial(kernel, line, chunks, heads_per, resp_per),
        out_shape=(
            jax.ShapeDtypeStruct(cotangent.shape, bf),
            jax.ShapeDtypeStruct(queries.shape, bf),
            jax.ShapeDtypeStruct(
                (head_devices, resp_per, key_count, key_cols // head_devices), bf
            ),
        ),
        grid=(chunks + line + 1,),
        in_specs=[
            pl.BlockSpec(memory_space=pltpu.SMEM),
            pl.BlockSpec((row_count, heads_per * q_cols), tile),
            pl.BlockSpec((row_count, heads_per * nope), tile),
            pl.BlockSpec(memory_space=pl.ANY),
            pl.BlockSpec(memory_space=pl.ANY),
            whole,
            whole,
        ],
        out_specs=(
            pl.BlockSpec((row_count, heads_per * nope), tile),
            pl.BlockSpec((row_count, heads_per * q_cols), tile),
            whole,
        ),
        scratch_shapes=[
            pltpu.VMEM((resp_per, key_count, key_cols), jnp.float32),
            pltpu.VMEM((2, line, 2, 2, head_count, slice_cols, nope), bf),
            pltpu.VMEM((line, 2, 2, prompt_rows, key_cols), bf),
            pltpu.VMEM((resp_per, key_count, key_cols), bf),
            pltpu.VMEM((resp_per, rows, key_cols), bf),
            pltpu.VMEM((resp_per, rows, latent), bf),
            pltpu.VMEM((heads_per, resp_per * tokens, latent), bf),
            pltpu.VMEM((heads_per, resp_per * tokens, key_cols), bf),
            pltpu.SemaphoreType.DMA((3,)),
            pltpu.SemaphoreType.DMA((chunks + 1, line - 1)),
            pltpu.SemaphoreType.DMA((chunks + 1, line - 1)),
            pltpu.SemaphoreType.DMA((chunks + 1, 4)),
            pltpu.SemaphoreType.DMA((chunks + 1, 4)),
            pltpu.SemaphoreType.DMA((chunks, 2 * line)),
            pltpu.SemaphoreType.DMA((chunks, 2 * line)),
        ],
        compiler_params=pltpu.CompilerParams(
            collective_id=0, has_side_effects=True, dimension_semantics=("arbitrary",)
        ),
    )(meta, queries, cotangent, wk, wv, prompt_latent, own_cols)


def tail_kernel(
    devices,
    head_devices,
    prompt_rows,
    slots,
    parts_ref,
    own_ref,
    prompt_out,
    head_in,
    out_rows,
    in_rows,
    out_sums,
    in_sums,
    head_send,
    head_recv,
    row_send,
    row_recv,
    sum_send,
    sum_recv,
):
    me = lax.axis_index("resp")
    mine = lax.axis_index("head")
    resp_per, key_count, share = parts_ref.shape[1:]
    tokens = key_count - prompt_rows
    piece = prompt_rows // devices

    def ahead(d):
        return lax.rem(me + d, devices)

    def behind(d):
        return lax.rem(me + devices - d, devices)

    barrier = pltpu.get_barrier_semaphore()
    for d in range(1, devices):
        pl.semaphore_signal(barrier, inc=1, device_id={"resp": ahead(d)}, device_id_type=MESH)
    for d in range(1, head_devices):
        peer = lax.rem(mine + d, head_devices)
        pl.semaphore_signal(barrier, inc=1, device_id={"head": peer}, device_id_type=MESH)
    pl.semaphore_wait(barrier, devices + head_devices - 2)

    def head_copy(d, slot):
        peer = lax.rem(mine + d, head_devices)
        return pltpu.make_async_remote_copy(
            src_ref=parts_ref.at[peer],
            dst_ref=head_in.at[slot],
            send_sem=head_send.at[d - 1],
            recv_sem=head_recv.at[d - 1],
            device_id={"head": peer},
            device_id_type=MESH,
        )

    def spread(source, target, send, recv, d, slot):
        return pltpu.make_async_remote_copy(
            src_ref=source.at[ahead(d)],
            dst_ref=target.at[slot],
            send_sem=send.at[d - 1],
            recv_sem=recv.at[d - 1],
            device_id={"resp": ahead(d)},
            device_id_type=MESH,
        )

    for d in range(1, head_devices):
        head_copy(d, mine).start()
    total = parts_ref[mine].astype(jnp.float32)
    for d in range(1, head_devices):
        source = lax.rem(mine + head_devices - d, head_devices)
        head_copy(d, source).wait_recv()
        total = total + head_in[source].astype(jnp.float32)
    for r in range(resp_per):
        for i in range(devices):
            out_rows[i, r * piece : (r + 1) * piece, :] = total[r, i * piece : (i + 1) * piece]
    for d in range(1, devices):
        spread(out_rows, in_rows, row_send, row_recv, d, me).start()
    in_rows[me] = out_rows[me]
    for r in range(resp_per):
        own_ref[r * tokens : (r + 1) * tokens, :] = total[r, prompt_rows:]
    for d in range(1, devices):
        spread(out_rows, in_rows, row_send, row_recv, d, behind(d)).wait_recv()
    slot_at = lax.broadcasted_iota(jnp.int32, (devices, devices), 0)
    for p in range(piece):
        summed = jnp.zeros((devices, share), jnp.float32)
        for r in range(resp_per):
            table = (slot_at == slots[r : r + 1, :]).astype(jnp.float32)
            summed = summed + lax.dot_general(
                table,
                in_rows[:, r * piece + p, :],
                NN,
                precision=lax.Precision.HIGHEST,
                preferred_element_type=jnp.float32,
            )
        out_sums[:, p, :] = summed
    for d in range(1, devices):
        spread(out_sums, in_sums, sum_send, sum_recv, d, me).start()
    in_sums[me] = out_sums[me]
    for d in range(1, devices):
        spread(out_sums, in_sums, sum_send, sum_recv, d, behind(d)).wait_recv()
    for i in range(devices):
        prompt_out[0, i * piece : (i + 1) * piece, :] = in_sums[i]
    for d in range(1, head_devices):
        head_copy(d, mine).wait_send()
    for d in range(1, devices):
        spread(out_rows, in_rows, row_send, row_recv, d, me).wait_send()
        spread(out_sums, in_sums, sum_send, sum_recv, d, me).wait_send()


def finish(parts, slots, resp_devices, prompt_rows):
    head_devices, resp_per, key_count, share = parts.shape
    piece = prompt_rows // resp_devices
    whole = pl.BlockSpec(memory_space=pltpu.VMEM)
    spread = pltpu.SemaphoreType.DMA((resp_devices - 1,))
    across = pltpu.SemaphoreType.DMA((max(head_devices - 1, 1),))
    f32 = jnp.float32
    return pl.pallas_call(
        functools.partial(tail_kernel, resp_devices, head_devices, prompt_rows),
        out_shape=(
            jax.ShapeDtypeStruct((resp_per * (key_count - prompt_rows), share), f32),
            jax.ShapeDtypeStruct((1, prompt_rows, share), f32),
        ),
        in_specs=[whole, whole],
        out_specs=(whole, whole),
        scratch_shapes=[
            pltpu.VMEM(parts.shape, parts.dtype),
            pltpu.VMEM((resp_devices, resp_per * piece, share), f32),
            pltpu.VMEM((resp_devices, resp_per * piece, share), f32),
            pltpu.VMEM((resp_devices, piece, share), f32),
            pltpu.VMEM((resp_devices, piece, share), f32),
            across,
            across,
            spread,
            spread,
            spread,
            spread,
        ],
        compiler_params=pltpu.CompilerParams(collective_id=1, has_side_effects=True),
    )(slots, parts)


def body(
    queries,
    resp_latent,
    prompt_latent,
    up_keys,
    up_values,
    cotangent,
    prompt_len,
    resp_len,
    resp_count,
    owner,
):
    resp_devices = lax.axis_size("resp")
    head_devices = lax.axis_size("head")
    my_index = lax.axis_index("resp")
    resp_total = resp_len.shape[0]
    per_device = resp_total // resp_devices
    prompt_rows = prompt_latent.shape[1]
    prompts = jnp.arange(resp_count.shape[0], dtype=jnp.int32)
    earlier = prompts[None, :] < prompts[:, None]
    starts = jnp.sum(jnp.where(earlier, resp_count[None, :], 0), axis=1)
    numbers = jnp.arange(resp_total, dtype=jnp.int32)
    prompt_of = jnp.sum((starts[None, :] <= numbers[:, None]).astype(jnp.int32), axis=1) - 1
    chosen = prompt_of[:, None] == jnp.arange(prompt_len.shape[0], dtype=jnp.int32)[None, :]
    slot_of = jnp.sum(jnp.where(chosen, owner[None, :], 0), axis=1)
    plen_of = jnp.sum(jnp.where(chosen, prompt_len[None, :], 0), axis=1)
    table = jnp.stack([slot_of // 4, (slot_of // 2) % 2, slot_of % 2, plen_of, resp_len], axis=1)
    meta = lax.dynamic_slice_in_dim(table, my_index * per_device, per_device)
    keys_t = jnp.swapaxes(up_keys, 1, 2)
    own_cols = resp_latent.T
    attended, grad_query, parts = fused(
        queries, cotangent, keys_t, up_values, prompt_latent, own_cols, meta, resp_devices, head_devices
    )
    slots = slot_of.reshape(resp_devices, per_device).T
    grad_own, at_owner = finish(parts, slots, resp_devices, prompt_rows)
    return attended, grad_query, grad_own, at_owner


def solution(mesh):
    placed = (
        P("resp", "head"),
        P("resp", None),
        P("resp", None, None),
        P("head", None, "resp"),
        P("head", "resp", None),
        P("resp", "head"),
        P(),
        P(),
        P(),
        P(),
    )
    return jax.shard_map(
        body,
        mesh=mesh,
        in_specs=placed,
        out_specs=(
            P("resp", "head"),
            P("resp", "head"),
            P("resp", "head"),
            P("resp", None, "head"),
        ),
        check_vma=False,
    )
```
